32 devices in a mesh: dp: 8 (over z, x), tensor: 4 (over y, core).
Axes of the slice: x: 2, y: 2, z: 4, core: 2. Of those that a mesh axis runs over, the one named last changes fastest.
Arguments:
- tokens: bfloat16 [16384, 768], P(('dp', 'tensor')), may hold values from -6 to 6
- seq_lengths: int32 [8, 3], P('dp'), may hold values from 0 to 2048, as said below
- norm1_gain: float32 [768], replicated, may hold values from 0.1 to 1.9
- norm1_shift: float32 [768], replicated, may hold values from -2 to 2
- qkv_weight: bfloat16 [768, 3, 768], P('dp', None, 'tensor'), may hold values from -0.21875 to 0.21875
- qv_bias: float32 [2, 768], replicated, may hold values from -3 to 3
- out_weight: bfloat16 [768, 768], P('tensor', 'dp'), may hold values from -0.875 to 0.875
- out_bias: float32 [768], replicated, may hold values from -2 to 2
- norm2_gain: float32 [768], replicated, may hold values from 0.1 to 1.9
- norm2_shift: float32 [768], replicated, may hold values from -2 to 2
- fc_weight: bfloat16 [768, 3072], P('dp', 'tensor'), may hold values from -0.21875 to 0.21875
- fc_bias: float32 [3072], replicated, may hold values from -3 to 3
- proj_weight: bfloat16 [3072, 768], P('tensor', 'dp'), may hold values from -0.109375 to 0.109375
- proj_bias: float32 [768], replicated, may hold values from -2 to 2
- out_grad: bfloat16 [16384, 768], P(('dp', 'tensor')), may hold values from -6 to 6
Outputs:
- block_out: bfloat16 [16384, 768], P(('dp', 'tensor'))
- grad_tokens: bfloat16 [16384, 768], P(('dp', 'tensor'))
- grad_norm1_gain: float32 [768], replicated
- grad_norm1_shift: float32 [768], replicated
- grad_qkv_weight: float32 [768, 3, 768], P('dp', None, 'tensor')
- grad_qv_bias: float32 [2, 768], replicated
- grad_out_weight: float32 [768, 768], P('tensor', 'dp')
- grad_out_bias: float32 [768], replicated
- grad_norm2_gain: float32 [768], replicated
- grad_norm2_shift: float32 [768], replicated
- grad_fc_weight: float32 [768, 3072], P('dp', 'tensor')
- grad_fc_bias: float32 [3072], replicated
- grad_proj_weight: float32 [3072, 768], P('tensor', 'dp')
- grad_proj_bias: float32 [768], replicated
The draws below stay inside these ranges and needn't reach their ends.
Inputs may be any that keep to these rules, and one draw needn't show every extreme that they name: `seq_lengths`: A group holds one to three sequences; its nonzero lengths fill the first slots; each is at least 512; rounded up to multiples of 128 they sum to at most 2048; some group holds a single sequence of exactly 2048.
All inputs are finite; a program needn't handle non-finite values.
Results may differ from the reference program's by a relative error of at most 0.015.
Values may be sent and summed in bfloat16 or wider, within the bound.
No kernel may reach another device: no remote copies, remote signals or barrier semaphores. Data moves between devices by JAX's collectives and lax.ppermute only.
A program may use at most 192 MiB of HBM per device.

```python
import jax
import jax.numpy as jnp
from jax import lax

D = 768
NH = 12
FF = 3072
HS = 64
SEQS = 3
BLK = 128
CAP = 2048
GROUPS = 8
TOKENS = 16384


def draw_seq_lengths(key, part):
    kind_key, size_key, full_key = jax.random.split(jax.random.fold_in(key, 11), 3)
    group_ids = jnp.arange(GROUPS, dtype=jnp.int32)
    kinds = jax.random.randint(kind_key, (GROUPS,), 0, 3)
    full_group = jax.random.randint(full_key, (), 0, GROUPS)
    kinds = jnp.where(group_ids == full_group, 0, kinds)
    lowest = jnp.array([CAP // 2, CAP // 4, CAP // 4], dtype=jnp.int32)[kinds]
    highest = jnp.array([CAP, CAP // 2, CAP // 3 // BLK * BLK], dtype=jnp.int32)[kinds]
    counts = jnp.array([1, 2, 3], dtype=jnp.int32)[kinds]
    raw_bits = jax.random.randint(size_key, (GROUPS, SEQS), 0, 1 << 20)
    lengths = lowest[:, None] + raw_bits % (highest - lowest + 1)[:, None]
    slots = jnp.arange(SEQS, dtype=jnp.int32)[None, :]
    lengths = jnp.where(slots < counts[:, None], lengths, 0)
    lengths = jnp.where((group_ids[:, None] == full_group) & (slots == 0), CAP, lengths)
    return lengths.astype(jnp.int32)


def with_spikes(values, rng, source, target, parts, factor):
    def block_of(position):
        return (jnp.arange(values.shape[position]) // (values.shape[position] // parts)).reshape((-1,) + (1,) * (values.ndim - 1 - position))

    near = jax.random.permutation(rng, parts)[block_of(target)]
    far = (block_of(target) + parts // 2) % parts
    return jnp.where((block_of(source) == near) | (block_of(source) == far), factor * values, values)


def block_scale(stream_key, extent, cuts, low, top_value):
    level = 1.0
    for axis_at, parts in cuts:
        draws = jax.random.uniform(jax.random.fold_in(jax.random.fold_in(stream_key, 6), axis_at), (parts,), jnp.float32, low / len(cuts), top_value / len(cuts))
        level = level * jnp.repeat(jnp.exp(draws), extent[axis_at] // parts).reshape((-1,) + (1,) * (len(extent) - 1 - axis_at))
    return level


def centred(own_key, shape, deviation, reach, cuts=(), kind=jnp.bfloat16):
    drawn = deviation * jax.random.normal(own_key, shape, jnp.float32)
    if cuts:
        drawn = drawn * block_scale(own_key, shape, cuts, -0.22, 0.18)
    return jnp.clip(drawn, -reach, reach).astype(kind)


def gaussian_with(stream_key, extent, scale, limit, cuts, heavy, kind=jnp.bfloat16):
    entries = scale * jax.random.normal(stream_key, extent, jnp.float32)
    if cuts:
        entries = entries * block_scale(stream_key, extent, cuts, -0.22, 0.18)
    return jnp.clip(with_spikes(entries, jax.random.fold_in(stream_key, 3), *heavy), -limit, limit).astype(kind)


def setup_inputs(seed: int = 0) -> dict:
    key_list = jax.random.split(jax.random.key(seed), 16)
    tokens = centred(key_list[0], (TOKENS, D), 1.0, 6.0, ((0, 32),))
    seq_lengths = draw_seq_lengths(jax.random.fold_in(key_list[15], 71), 0)
    norm1_gain = jnp.clip(1.0 + 0.18 * jax.random.normal(key_list[2], (D,), jnp.float32), 0.1, 1.9)
    norm1_shift = centred(key_list[3], (D,), 0.3, 2.0, (), jnp.float32)
    qkv_weight = centred(key_list[4], (D, 3, D), D ** -0.5, 0.21875, ((0, 8), (2, 4)))
    qv_bias = centred(key_list[5], (2, D), 0.5, 3.0, (), jnp.float32)
    out_weight = centred(key_list[6], (D, D), (D // 16) ** -0.5, 0.875, ((0, 4), (1, 8)))
    out_bias = centred(key_list[7], (D,), 0.3, 2.0, (), jnp.float32)
    norm2_gain = jnp.clip(1.0 + 0.18 * jax.random.normal(key_list[8], (D,), jnp.float32), 0.1, 1.9)
    norm2_shift = centred(key_list[9], (D,), 0.3, 2.0, (), jnp.float32)
    fc_weight = centred(key_list[10], (D, FF), D ** -0.5, 0.21875, ((0, 8), (1, 4)))
    fc_bias = centred(key_list[11], (FF,), 0.5, 3.0, (), jnp.float32)
    proj_weight = centred(key_list[12], (FF, D), FF ** -0.5, 0.109375, ((0, 4), (1, 8)))
    proj_bias = centred(key_list[13], (D,), 0.3, 2.0, (), jnp.float32)
    out_grad = gaussian_with(key_list[14], (TOKENS, D), 1.0, 6.0, ((0, 32),), (0, 1, 32, 2.75))
    return dict(tokens=tokens, seq_lengths=seq_lengths, norm1_gain=norm1_gain, norm1_shift=norm1_shift, qkv_weight=qkv_weight, qv_bias=qv_bias, out_weight=out_weight, out_bias=out_bias, norm2_gain=norm2_gain, norm2_shift=norm2_shift, fc_weight=fc_weight, fc_bias=fc_bias, proj_weight=proj_weight, proj_bias=proj_bias, out_grad=out_grad)


EPSILON = 1e-05
MASKED = -1e+30
GELU_SCALE = 0.7978845608028654
exact_mode = lax.Precision.HIGHEST

@jax.custom_vjp
def low(v):
    return lax.optimization_barrier(v.astype(jnp.bfloat16)).astype(jnp.float32)

@jax.custom_vjp
def low_back(v):
    return v

def low_keep(v):
    return (low(v), None)

def low_pass(kept, grad):
    return (grad,)

def back_keep(v):
    return (v, None)

def back_low(kept, grad):
    return (low(grad),)
low.defvjp(low_keep, low_pass)
low_back.defvjp(back_keep, back_low)

def layer_norm(values, norm_gain, norm_shift):
    centre = values - lax.optimization_barrier(jnp.mean(values, axis=-1, keepdims=True))
    spread = lax.optimization_barrier(jnp.mean(centre * centre, axis=-1, keepdims=True))
    return centre * lax.rsqrt(spread + EPSILON) * norm_gain + norm_shift

def gelu_tanh(values):
    return 0.5 * values * (1.0 + jnp.tanh(GELU_SCALE * (values + 0.044715 * values * values * values)))

def segment_ids(lengths, capacity):
    padded = (lengths + BLK - 1) // BLK * BLK
    starts = jnp.cumsum(padded, axis=1) - padded
    places = jnp.arange(capacity, dtype=jnp.int32)
    inside = (places[None, None, :] >= starts[:, :, None]) & (places[None, None, :] < (starts + lengths)[:, :, None])
    labels = jnp.arange(lengths.shape[1], dtype=jnp.int32)[None, :, None] + 1
    return (lax.optimization_barrier(jnp.sum(jnp.where(inside, labels, 0), axis=1)) - 1).astype(jnp.int32)

def one_head(inputs):
    queries, key_rows, vals, labels = inputs
    places = jnp.arange(CAP, dtype=jnp.int32)
    raw_scores = low_back(jnp.dot(queries, key_rows.T, precision=exact_mode, preferred_element_type=jnp.float32) * HS ** (-0.5))
    allowed = (labels[:, None] == labels[None, :]) & (places[None, :] <= places[:, None]) & (labels[:, None] >= 0)
    scores = jnp.where(allowed, raw_scores, MASKED)
    row_peak = lax.optimization_barrier(jnp.max(scores, axis=-1, keepdims=True))
    weights = jnp.exp(scores - row_peak)
    probability = weights / lax.optimization_barrier(jnp.sum(weights, axis=-1, keepdims=True))
    return jnp.dot(low(probability), vals, precision=exact_mode, preferred_element_type=jnp.float32)

def split_heads(array):
    return array.reshape(GROUPS, CAP, NH, HS).transpose(0, 2, 1, 3).reshape(GROUPS * NH, CAP, HS)

def attend(queries, key_rows, vals, seg):
    labels = jnp.repeat(seg, NH, axis=0)
    result = lax.map(jax.checkpoint(one_head), (split_heads(queries), split_heads(key_rows), split_heads(vals), labels))
    return result.reshape(GROUPS, NH, CAP, HS).transpose(0, 2, 1, 3).reshape(GROUPS * CAP, NH * HS)

def reference(tokens, seq_lengths, norm1_gain, norm1_shift, qkv_weight, qv_bias, out_weight, out_bias, norm2_gain, norm2_shift, fc_weight, fc_bias, proj_weight, proj_bias, out_grad):
    seg = segment_ids(seq_lengths, CAP)
    live_rows = (seg >= 0).reshape(-1)

    def forward(stream, gain_one, shift_one, weight_qkv, bias_qv, weight_out, bias_out, gain_two, shift_two, weight_fc, bias_fc, weight_proj, bias_proj):
        first_norm = low(layer_norm(stream, gain_one, shift_one))
        projected = jnp.einsum('td,dcf->tcf', first_norm, weight_qkv, precision=exact_mode)
        queries = low(low_back(projected[:, 0] + bias_qv[0]))
        key_rows = low(low_back(projected[:, 1]))
        vals = low(low_back(projected[:, 2] + bias_qv[1]))
        attended = low(low_back(attend(queries, key_rows, vals, seg)))
        branch = low_back(jnp.dot(attended, weight_out, precision=exact_mode, preferred_element_type=jnp.float32) + bias_out)
        middle = stream + branch
        second_norm = low(layer_norm(middle, gain_two, shift_two))
        pre_gelu = low_back(jnp.dot(second_norm, weight_fc, precision=exact_mode, preferred_element_type=jnp.float32) + bias_fc)
        activated = low(gelu_tanh(pre_gelu))
        mlp_out = jnp.dot(activated, weight_proj, precision=exact_mode, preferred_element_type=jnp.float32) + bias_proj
        return jnp.where(live_rows[:, None], middle + mlp_out, 0.0)
    primals = (tokens.astype(jnp.float32), norm1_gain, norm1_shift, qkv_weight.astype(jnp.float32), qv_bias, out_weight.astype(jnp.float32), out_bias, norm2_gain, norm2_shift, fc_weight.astype(jnp.float32), fc_bias, proj_weight.astype(jnp.float32), proj_bias)
    result, pullback = jax.vjp(forward, *primals)
    grads = pullback(out_grad.astype(jnp.float32))
    return (result.astype(jnp.bfloat16), grads[0].astype(jnp.bfloat16), grads[1], grads[2], grads[3], grads[4], grads[5], grads[6], grads[7], grads[8], grads[9], grads[10], grads[11], grads[12])
```

```python
import jax
import jax.numpy as jnp
from jax import lax
from jax.sharding import PartitionSpec as P

HS = 64
BLK = 128
QB = 512


EPSILON = 1e-05
MASKED = -1e30
GELU_SCALE = 0.7978845608028654

BF = jnp.bfloat16
F32 = jnp.float32


def layer_norm(values, norm_gain, norm_shift):
    centre = values - jnp.mean(values, axis=-1, keepdims=True)
    spread = jnp.mean(centre * centre, axis=-1, keepdims=True)
    return centre * lax.rsqrt(spread + EPSILON) * norm_gain + norm_shift


def gelu_tanh(values):
    return (
        0.5 * values * (1.0 + jnp.tanh(GELU_SCALE * (values + 0.044715 * values * values * values)))
    )


def segment_ids(lengths, capacity):
    padded = (lengths + BLK - 1) // BLK * BLK
    starts = jnp.cumsum(padded, axis=1) - padded
    places = jnp.arange(capacity, dtype=jnp.int32)
    inside = (places[None, None, :] >= starts[:, :, None]) & (
        places[None, None, :] < (starts + lengths)[:, :, None]
    )
    labels = jnp.arange(lengths.shape[1], dtype=jnp.int32)[None, :, None] + 1
    return jnp.sum(jnp.where(inside, labels, 0), axis=1) - 1


def swap(value, axis, bits):
    size = lax.axis_size(axis)
    return lax.ppermute(value, axis, [(i, i ^ bits) for i in range(size)])


def bits_of(axis):
    size = lax.axis_size(axis)
    count = size.bit_length() - 1
    assert 1 << count == size
    return [1 << b for b in range(count)]


def gather_rows(shard, axis):
    here = lax.axis_index(axis)
    full = shard[None]
    for bit in reversed(bits_of(axis)):
        other = swap(full, axis, bit)
        high = (here & bit) > 0
        full = jnp.where(
            high, jnp.stack([other, full], 1), jnp.stack([full, other], 1)
        ).reshape(-1, *shard.shape)
    return full


def scatter_sum(part, axis):
    here = lax.axis_index(axis)
    for bit in bits_of(axis):
        high = ((here & bit) > 0).astype(jnp.int32)
        pairs = part.reshape(-1, 2, *part.shape[1:])
        keep = lax.dynamic_index_in_dim(pairs, high, 1, keepdims=False)
        give = lax.dynamic_index_in_dim(pairs, 1 - high, 1, keepdims=False)
        part = keep.astype(F32) + swap(give.astype(BF), axis, bit).astype(F32)
    return part[0]


def relative_gather(rows, axis):
    placed = {0: rows}
    for bit in reversed(bits_of(axis)):
        placed.update({r ^ bit: swap(b, axis, bit) for r, b in list(placed.items())})
    return [placed[r] for r in range(len(placed))]


def relative_scatter(blocks, axis):
    live = {r: b for r, b in enumerate(blocks)}
    for bit in bits_of(axis):
        fresh = {}
        for r in sorted(live):
            if not r & bit:
                got = swap(live[r | bit].astype(BF), axis, bit)
                fresh[r] = live[r].astype(F32) + got.astype(F32)
        live = fresh
    return live[0]


def exchange(blocks, axis):
    return [b if r == 0 else swap(b, axis, r) for r, b in enumerate(blocks)]


def everyone_sum(value, axes):
    for axis in axes:
        for bit in bits_of(axis):
            value = value + swap(value, axis, bit)
    return value


def absolute(blocks, axis):
    here = lax.axis_index(axis)
    rows = blocks[0].shape[0]
    full = jnp.zeros((rows * len(blocks), *blocks[0].shape[1:]), blocks[0].dtype)
    for r, b in enumerate(blocks):
        full = lax.dynamic_update_slice_in_dim(full, b, (here ^ r) * rows, 0)
    return full


def block_scores(queries, key_rows, seg_query, seg_key, place_query, place_key):
    raw_scores = jnp.einsum(
        "qhd,khd->hqk", queries, key_rows, preferred_element_type=jnp.float32
    ) * HS ** (-0.5)
    allowed = (
        (seg_query[:, None] == seg_key[None, :])
        & (place_key[None, :] <= place_query[:, None])
        & (seg_query[:, None] >= 0)
    )
    return jnp.where(allowed[None], raw_scores, MASKED)


def attention_forward(queries, key_rows, values, seg):
    capacity = queries.shape[0]
    places = jnp.arange(capacity, dtype=jnp.int32)
    outputs = []
    log_totals = []
    for block_begin in range(0, capacity, QB):
        block_end = block_begin + QB
        scores = block_scores(
            queries[block_begin:block_end],
            key_rows[:block_end],
            seg[block_begin:block_end],
            seg[:block_end],
            places[block_begin:block_end],
            places[:block_end],
        )
        row_peak = jnp.max(scores, axis=-1, keepdims=True)
        weights = jnp.exp(scores - row_peak)
        row_total = jnp.sum(weights, axis=-1, keepdims=True)
        probability = (weights / row_total).astype(BF)
        outputs.append(
            jnp.einsum("hqk,khd->qhd", probability, values[:block_end], preferred_element_type=F32)
        )
        log_totals.append(row_peak + jnp.log(row_total))
    return jnp.concatenate(outputs, 0).astype(BF), jnp.concatenate(log_totals, 1)


def attention_backward(queries, key_rows, values, seg, log_total, grad_attended):
    capacity = queries.shape[0]
    scale = HS ** (-0.5)
    places = jnp.arange(capacity, dtype=jnp.int32)
    query_grads = []
    grad_keys = jnp.zeros(key_rows.shape, F32)
    grad_values = jnp.zeros(values.shape, F32)
    for block_begin in range(0, capacity, QB):
        block_end = block_begin + QB
        query_block = queries[block_begin:block_end]
        attended_grad_block = grad_attended[block_begin:block_end]
        scores = block_scores(
            query_block,
            key_rows[:block_end],
            seg[block_begin:block_end],
            seg[:block_end],
            places[block_begin:block_end],
            places[:block_end],
        )
        probability = jnp.exp(scores - log_total[:, block_begin:block_end])
        grad_probs = jnp.einsum(
            "qhd,khd->hqk", attended_grad_block, values[:block_end], preferred_element_type=F32
        )
        centre = jnp.sum(grad_probs * probability, axis=-1, keepdims=True)
        grad_scores = (probability * (grad_probs - centre)).astype(BF)
        query_grads.append(
            jnp.einsum("hqk,khd->qhd", grad_scores, key_rows[:block_end], preferred_element_type=F32)
            * scale
        )
        grad_keys = grad_keys.at[:block_end].add(
            jnp.einsum("hqk,qhd->khd", grad_scores, query_block, preferred_element_type=F32) * scale
        )
        grad_values = grad_values.at[:block_end].add(
            jnp.einsum(
                "hqk,qhd->khd", probability.astype(BF), attended_grad_block, preferred_element_type=F32
            )
        )
    return jnp.concatenate(query_grads, 0), grad_keys, grad_values


def per_device(
    tokens,
    seq_lengths,
    norm1_gain,
    norm1_shift,
    qkv_weight,
    qv_bias,
    out_weight,
    out_bias,
    norm2_gain,
    norm2_shift,
    fc_weight,
    fc_bias,
    proj_weight,
    proj_bias,
    out_grad,
):
    tensor_size = lax.axis_size("tensor")
    dp_size = lax.axis_size("dp")
    tensor_pos = lax.axis_index("tensor")
    local_rows, model_width = tokens.shape
    capacity = local_rows * tensor_size
    shard_rows = qkv_weight.shape[0]
    head_cols = qkv_weight.shape[2]
    hidden_cols = fc_weight.shape[1]

    full_qkv = gather_rows(qkv_weight.reshape(shard_rows, 3 * head_cols), "dp").reshape(
        model_width, 3 * head_cols
    )
    out_turned = gather_rows(out_weight.T, "dp").reshape(model_width, head_cols)
    fc_cols = gather_rows(fc_weight, "dp").reshape(model_width, hidden_cols)
    proj_turned = gather_rows(proj_weight.T, "dp").reshape(model_width, hidden_cols)
    outs = relative_gather(out_turned, "tensor")

    seg = segment_ids(seq_lengths, capacity)[0]
    live_here = lax.dynamic_slice_in_dim(seg, tensor_pos * local_rows, local_rows, 0) >= 0
    stream = tokens.astype(F32)
    first_norm, first_back = jax.vjp(layer_norm, stream, norm1_gain, norm1_shift)
    firsts = relative_gather(first_norm.astype(BF), "tensor")
    first_all = absolute(firsts, "tensor")
    grad_mlp = jnp.where(live_here[:, None], out_grad, jnp.zeros_like(out_grad))
    grads = relative_gather(grad_mlp, "tensor")

    projected = jnp.dot(first_all, full_qkv, preferred_element_type=F32).reshape(
        capacity, 3, head_cols
    )
    bias_here = lax.dynamic_slice_in_dim(qv_bias, tensor_pos * head_cols, head_cols, 1)
    queries = (projected[:, 0] + bias_here[0]).astype(BF).reshape(capacity, -1, HS)
    key_rows = projected[:, 1].astype(BF).reshape(capacity, -1, HS)
    values = (projected[:, 2] + bias_here[1]).astype(BF).reshape(capacity, -1, HS)
    attended, log_total = attention_forward(queries, key_rows, values, seg)
    attended = attended.reshape(capacity, head_cols)

    mine = exchange(
        [
            lax.dynamic_slice_in_dim(attended, (tensor_pos ^ r) * local_rows, local_rows, 0)
            for r in range(tensor_size)
        ],
        "tensor",
    )
    branch = sum(
        jnp.einsum("tc,dc->td", a, w, preferred_element_type=F32) for a, w in zip(mine, outs, strict=True)
    )
    middle = stream + branch + out_bias
    second_norm, second_back = jax.vjp(layer_norm, middle, norm2_gain, norm2_shift)
    second_all = jnp.concatenate(relative_gather(second_norm.astype(BF), "tensor"), 0)
    grad_all = jnp.concatenate(grads, 0)
    fc_bias_here = lax.dynamic_slice_in_dim(fc_bias, tensor_pos * hidden_cols, hidden_cols, 0)
    pre_gelu = jnp.dot(second_all, fc_cols, preferred_element_type=F32) + fc_bias_here
    activated_f, gelu_back = jax.vjp(gelu_tanh, pre_gelu)
    activated = activated_f.astype(BF)
    grad_act = jnp.dot(grad_all, proj_turned, preferred_element_type=F32)
    grad_pre = gelu_back(grad_act)[0].astype(BF)
    grad_second_part = jnp.einsum("tf,df->td", grad_pre, fc_cols, preferred_element_type=F32).astype(
        BF
    )
    grad_second = relative_scatter(
        list(grad_second_part.reshape(tensor_size, local_rows, model_width)), "tensor"
    )
    mlp_part = jnp.einsum("tf,df->td", activated, proj_turned, preferred_element_type=F32).astype(BF)
    mlp_out = relative_scatter(
        list(mlp_part.reshape(tensor_size, local_rows, model_width)), "tensor"
    )
    result = jnp.where(live_here[:, None], middle + mlp_out + proj_bias, 0.0).astype(BF)

    grad_here = grad_mlp.astype(F32)
    grad_proj = jnp.einsum("td,tf->df", grad_all, activated, preferred_element_type=F32)
    grad_fc = jnp.einsum("td,tf->df", second_all, grad_pre, preferred_element_type=F32)
    grad_fc_cols = jnp.sum(grad_pre.astype(F32), axis=0)
    sum_fc = scatter_sum(grad_fc.reshape(dp_size, shard_rows, hidden_cols), "dp")
    sum_proj = scatter_sum(grad_proj.reshape(dp_size, shard_rows, hidden_cols), "dp").T

    middle_part, grad_gain_two, grad_shift_two = second_back(grad_second)
    grad_middle = grad_here + middle_part
    grad_branch = grad_middle.astype(BF)
    grad_mine = [
        jnp.dot(grad_branch, w, preferred_element_type=F32).astype(BF) for w in outs
    ]
    grad_attended = absolute(exchange(grad_mine, "tensor"), "tensor").reshape(capacity, -1, HS)
    grad_out_parts = exchange(
        [
            jnp.einsum("td,tc->dc", grad_branch, a, preferred_element_type=F32).astype(BF)
            for a in mine
        ],
        "tensor",
    )
    grad_out = sum(g.astype(F32) for g in grad_out_parts)
    sum_out = scatter_sum(grad_out.reshape(dp_size, shard_rows, head_cols), "dp").T

    grad_queries, grad_keys, grad_values = attention_backward(
        queries, key_rows, values, seg, log_total, grad_attended
    )
    grad_qkv = (
        jnp.stack([grad_queries, grad_keys, grad_values], 1)
        .reshape(capacity, 3 * head_cols)
        .astype(BF)
    )
    grad_first_part = jnp.einsum("tc,dc->td", grad_qkv, full_qkv, preferred_element_type=F32).astype(
        BF
    )
    grad_first = scatter_sum(
        grad_first_part.reshape(tensor_size, local_rows, model_width), "tensor"
    )
    grad_qkv_w = jnp.einsum("td,tc->dc", first_all, grad_qkv, preferred_element_type=F32)
    sum_qkv = scatter_sum(grad_qkv_w.reshape(dp_size, shard_rows, 3 * head_cols), "dp").reshape(
        shard_rows, 3, head_cols
    )
    grad_bias_cols = jnp.sum(grad_qkv.reshape(capacity, 3, head_cols).astype(F32), axis=0)[0::2]
    input_part, grad_gain_one, grad_shift_one = first_back(grad_first)
    grad_tokens = (grad_middle + input_part).astype(BF)

    qv_full = lax.dynamic_update_slice_in_dim(
        jnp.zeros((2, model_width), F32), grad_bias_cols, tensor_pos * head_cols, 1
    )
    fc_full = lax.dynamic_update_slice_in_dim(
        jnp.zeros(fc_bias.shape, F32), grad_fc_cols, tensor_pos * hidden_cols, 0
    )
    out_bias_part = jnp.sum(grad_branch.astype(F32), axis=0)
    proj_bias_part = jnp.sum(grad_here, axis=0)
    early = everyone_sum(
        jnp.concatenate(
            [out_bias_part, grad_gain_two, grad_shift_two, proj_bias_part, fc_full]
        ).reshape(-1, 128),
        ("tensor", "dp"),
    ).reshape(-1)
    late = everyone_sum(
        jnp.concatenate([grad_gain_one, grad_shift_one, qv_full.reshape(-1)]).reshape(-1, 128),
        ("tensor", "dp"),
    ).reshape(-1)
    w = model_width
    return (
        result,
        grad_tokens,
        late[:w],
        late[w : 2 * w],
        sum_qkv,
        late[2 * w :].reshape(2, w),
        sum_out,
        early[:w],
        early[w : 2 * w],
        early[2 * w : 3 * w],
        sum_fc,
        early[4 * w :],
        sum_proj,
        early[3 * w : 4 * w],
    )


def solution(mesh):
    placed = (
        P(("dp", "tensor"), None),
        P("dp", None),
        P(),
        P(),
        P("dp", None, "tensor"),
        P(),
        P("tensor", "dp"),
        P(),
        P(),
        P(),
        P("dp", "tensor"),
        P(),
        P("tensor", "dp"),
        P(),
        P(("dp", "tensor"), None),
    )
    return jax.shard_map(
        per_device,
        mesh=mesh,
        in_specs=placed,
        out_specs=(
            P(("dp", "tensor"), None),
            P(("dp", "tensor"), None),
            P(),
            P(),
            P("dp", None, "tensor"),
            P(),
            P("tensor", "dp"),
            P(),
            P(),
            P(),
            P("dp", "tensor"),
            P(),
            P("tensor", "dp"),
            P(),
        ),
        check_vma=False,
    )
```

```python
import functools

import jax
import jax.numpy as jnp
from jax import lax
from jax.experimental import pallas as pl
from jax.experimental.pallas import tpu as pltpu
from jax.sharding import PartitionSpec as P

HS = 64
BLK = 128


EPSILON = 1e-05
MASKED = -1e30
GELU_SCALE = 0.7978845608028654

BF = jnp.bfloat16
F32 = jnp.float32


def segment_ids(lengths, capacity):
    padded = (lengths + BLK - 1) // BLK * BLK
    starts = jnp.cumsum(padded, axis=1) - padded
    places = jnp.arange(capacity, dtype=jnp.int32)
    inside = (places[None, None, :] >= starts[:, :, None]) & (
        places[None, None, :] < (starts + lengths)[:, :, None]
    )
    labels = jnp.arange(lengths.shape[1], dtype=jnp.int32)[None, :, None] + 1
    return jnp.sum(jnp.where(inside, labels, 0), axis=1) - 1


def swap(value, axis, bits):
    size = lax.axis_size(axis)
    return lax.ppermute(value, axis, [(i, i ^ bits) for i in range(size)])


def bits_of(axis):
    size = lax.axis_size(axis)
    count = size.bit_length() - 1
    assert 1 << count == size
    return [1 << b for b in range(count)]


def after(value, *others):
    return lax.optimization_barrier((value, *others))[0]


def gather_step(full, axis, bit, other=None):
    high = (lax.axis_index(axis) & bit) > 0
    other = swap(full, axis, bit) if other is None else other
    return jnp.where(
        high, jnp.stack([other, full], 1), jnp.stack([full, other], 1)
    ).reshape(-1, *full.shape[1:])


def exchange(blocks, axis):
    return [b if r == 0 else swap(b, axis, r) for r, b in enumerate(blocks)]


def everyone_sum(value, axes):
    for axis in axes:
        for bit in bits_of(axis):
            value = value + swap(value, axis, bit)
    return value


def first_keys(seg, slots):
    places = jnp.arange(seg.shape[0], dtype=jnp.int32)
    begins = jnp.where(seg != jnp.concatenate([jnp.full((1,), -2, jnp.int32), seg[:-1]]), places, 0)
    labels = jnp.arange(slots, dtype=jnp.int32)
    starts = jnp.sum(jnp.where((seg[None] == labels[:, None]), begins[None], 0), axis=1)
    mine = jnp.sum(jnp.where(seg[:, None] == labels[None], starts[None], 0), axis=1)
    return jnp.where(seg >= 0, mine, places)


def nt(a, b):
    return lax.dot_general(a, b, (((1,), (1,)), ((), ())), preferred_element_type=F32)


def nn(a, b):
    return lax.dot_general(a, b, (((1,), (0,)), ((), ())), preferred_element_type=F32)


def tn(a, b):
    return lax.dot_general(a, b, (((0,), (0,)), ((), ())), preferred_element_type=F32)


def rows_at(block, size):
    return pl.ds(pl.multiple_of(block * size, size), size)


def masked_scores(keys, queries, low, first_key, first_query):
    scores = nt(keys, queries)
    key_at = lax.broadcasted_iota(jnp.int32, scores.shape, 0) + first_key
    query_at = lax.broadcasted_iota(jnp.int32, (1, scores.shape[1]), 1) + first_query
    return jnp.where((key_at >= low) & (key_at <= query_at), scores, MASKED)


def forward_kernel(heads, block, here_ref, start_ref, low_ref, *refs):
    count = here_ref.shape[0] - 1
    token_refs = refs[:count]
    weight_ref, bias_ref, gain_ref, shift_ref = refs[count : count + 4]
    (h1_ref, hat_ref, q_ref, k_ref, v_ref, out_ref, lse_ref, send_ref) = refs[count + 4 :]
    here = here_ref[count]
    local_rows = token_refs[0].shape[0]
    chunk = 256
    for r in range(count):

        def project(step, carry, r=r):
            base = pl.multiple_of((here_ref[r]) * local_rows + step * chunk, chunk)
            rows = token_refs[r][rows_at(step, chunk), :].astype(F32)
            centre = rows - jnp.mean(rows, axis=-1, keepdims=True)
            spread = jnp.mean(centre * centre, axis=-1, keepdims=True)
            hat = centre * lax.rsqrt(spread + EPSILON)
            h1 = (hat * gain_ref[...] + shift_ref[...]).astype(BF)
            hat_ref[pl.ds(base, chunk), :] = hat.astype(BF)
            h1_ref[pl.ds(base, chunk), :] = h1
            qkv = (nn(h1, weight_ref[...]) + bias_ref[...]).astype(BF)
            for h in range(heads):
                at = 3 * h * HS
                q_ref[h, pl.ds(base, chunk), :] = qkv[:, at : at + HS] * HS ** (-0.5)
                k_ref[h, pl.ds(base, chunk), :] = qkv[:, at + HS : at + 2 * HS]
                v_ref[h, pl.ds(base, chunk), :] = qkv[:, at + 2 * HS : at + 3 * HS]
            return carry

        lax.fori_loop(0, local_rows // chunk, project, 0)

    blocks = q_ref.shape[1] // block

    def query_step(i, carry):
        low = low_ref[0:1, rows_at(i, block)]

        def key_step(j, state):
            fresh = []
            for h in range(heads):
                peak, total, acc = state[3 * h : 3 * h + 3]
                scores = masked_scores(
                    k_ref[h, rows_at(j, block), :],
                    q_ref[h, rows_at(i, block), :],
                    low,
                    j * block,
                    i * block,
                )
                peak_now = jnp.maximum(peak, jnp.max(scores, axis=0, keepdims=True))
                decay = jnp.exp(peak - peak_now)
                weights = jnp.exp(scores - peak_now)
                total = total * decay + jnp.sum(weights, axis=0, keepdims=True)
                acc = acc * decay + tn(v_ref[h, rows_at(j, block), :], weights.astype(BF))
                fresh += [peak_now, total, acc]
            return tuple(fresh)

        init = (
            jnp.full((1, block), MASKED, F32),
            jnp.zeros((1, block), F32),
            jnp.zeros((HS, block), F32),
        ) * heads
        state = lax.fori_loop(start_ref[i], i + 1, key_step, init)
        slot = lax.bitwise_xor(i, here)
        for h in range(heads):
            peak, total, acc = state[3 * h : 3 * h + 3]
            rows = acc / total
            out_ref[h, :, rows_at(i, block)] = rows
            lse_ref[h, :, rows_at(i, block)] = peak + jnp.log(total)
            send_ref[slot, h * HS : (h + 1) * HS, :] = rows.astype(BF)
        return carry

    lax.fori_loop(0, blocks, query_step, 0)


def attention_forward(blocks, weight, bias, gain, shift, low, starts, order, heads):
    rows, width = blocks[0].shape
    count = len(blocks)
    total = rows * count
    flops = 2 * total * width * weight.shape[1] + 2 * heads * total * total * HS
    return pl.pallas_call(
        functools.partial(forward_kernel, heads, rows),
        out_shape=(
            shape((total, width), BF),
            shape((total, width), BF),
            shape((heads, total, HS), BF),
            shape((heads, total, HS), BF),
            shape((heads, total, HS), BF),
            shape((heads, HS, total), F32),
            shape((heads, 1, total), F32),
            shape((count, heads * HS, rows), BF),
        ),
        in_specs=[pl.BlockSpec(memory_space=pltpu.SMEM)] * 2
        + [pl.BlockSpec(memory_space=pltpu.VMEM)] * (count + 5),
        out_specs=[pl.BlockSpec(memory_space=pltpu.VMEM)] * 8,
        compiler_params=pltpu.CompilerParams(vmem_limit_bytes=60000 * 1024),
        cost_estimate=pl.CostEstimate(
            flops=flops, bytes_accessed=24 << 20, transcendentals=heads * total * total // 2
        ),
        name="attention_forward",
    )(order, starts, low, *blocks, weight, bias, gain, shift)


def backward_kernel(
    first_head, heads, block, start_ref, order_ref, low_ref, q_ref, k_ref, v_ref, out_ref, lse_ref, *refs
):
    count = order_ref.shape[0] - 1
    grad_refs = refs[:count]
    result_ref = refs[count]
    grad_t_ref, grad_ref, centre_ref, dk_ref, dv_ref, kt_ref, dq_ref = refs[count + 1 :]
    for r in range(count):
        for h in range(heads):
            whole = first_head + h
            piece = grad_refs[r][whole * HS : (whole + 1) * HS, :]
            at = rows_at(order_ref[r], block)
            grad_t_ref[h, :, at] = piece
            grad_ref[h, at, :] = piece.T
            centre_ref[h, :, at] = jnp.sum(
                piece.astype(F32) * out_ref[whole, :, at], axis=0, keepdims=True
            )
            kt_ref[h, :, r * block : (r + 1) * block] = k_ref[
                whole, r * block : (r + 1) * block, :
            ].T
    dk_ref[...] = jnp.zeros_like(dk_ref)
    dv_ref[...] = jnp.zeros_like(dv_ref)
    blocks = q_ref.shape[1] // block

    def query_step(i, carry):
        here = rows_at(i, block)
        low = low_ref[0:1, here]

        def key_step(j, state):
            there = rows_at(j, block)
            fresh = []
            for h in range(heads):
                whole = first_head + h
                queries = q_ref[whole, here, :]
                scores = masked_scores(k_ref[whole, there, :], queries, low, j * block, i * block)
                probs = jnp.exp(scores - lse_ref[whole, :, here])
                grad_probs = nn(v_ref[whole, there, :], grad_t_ref[h, :, here])
                grad_scores = (probs * (grad_probs - centre_ref[h, :, here])).astype(BF)
                dv_ref[h, there, :] += nn(probs.astype(BF), grad_ref[h, here, :])
                dk_ref[h, there, :] += nn(grad_scores, queries)
                fresh.append(state[h] + nn(kt_ref[h, :, there], grad_scores))
            return tuple(fresh)

        state = lax.fori_loop(
            start_ref[i], i + 1, key_step, (jnp.zeros((HS, block), F32),) * heads
        )
        for h in range(heads):
            dq_ref[h, here, :] = (state[h] * HS ** (-0.5)).T.astype(BF)
        return carry

    lax.fori_loop(0, blocks, query_step, 0)

    def finish(i, carry):
        here = rows_at(i, block)
        pieces = []
        for h in range(heads):
            pieces += [dq_ref[h, here, :], dk_ref[h, here, :].astype(BF), dv_ref[h, here, :].astype(BF)]
        result_ref[here, :] = jnp.concatenate(pieces, axis=1)
        return carry

    lax.fori_loop(0, blocks, finish, 0)


def vmem(count):
    return [pl.BlockSpec(memory_space=pltpu.VMEM)] * count


def smem(count):
    return [pl.BlockSpec(memory_space=pltpu.SMEM)] * count


def kernel_call(body, name, out_shape, scalars, arrays, flops, scratch=(), transcendentals=0):
    moved = sum(a.size * a.dtype.itemsize for a in arrays) + sum(
        o.size * jnp.dtype(o.dtype).itemsize for o in out_shape
    )
    return pl.pallas_call(
        body,
        out_shape=tuple(out_shape),
        in_specs=smem(len(scalars)) + vmem(len(arrays)),
        out_specs=vmem(len(out_shape)),
        scratch_shapes=list(scratch),
        compiler_params=pltpu.CompilerParams(vmem_limit_bytes=60000 * 1024),
        cost_estimate=pl.CostEstimate(
            flops=flops, bytes_accessed=moved, transcendentals=transcendentals
        ),
        name=name,
    )(*scalars, *arrays)


def shape(dims, kind):
    return jax.ShapeDtypeStruct(dims, kind)


def attention_backward(first_head, heads, q, k, v, out, lse, grads, low, starts, order):
    total = q.shape[1]
    rows = total // len(grads)
    return kernel_call(
        functools.partial(backward_kernel, first_head, heads, rows),
        "attention_backward",
        [shape((total, 3 * HS * heads), BF)],
        [starts, order],
        [low, q, k, v, out, lse, *grads],
        5 * heads * total * total * HS,
        [
            pltpu.VMEM((heads, HS, total), BF),
            pltpu.VMEM((heads, total, HS), BF),
            pltpu.VMEM((heads, 1, total), F32),
            pltpu.VMEM((heads, total, HS), F32),
            pltpu.VMEM((heads, total, HS), F32),
            pltpu.VMEM((heads, HS, total), BF),
            pltpu.VMEM((heads, total, HS), BF),
        ],
        heads * total * total // 2,
    )


def normalised(rows):
    centre = rows - jnp.mean(rows, axis=-1, keepdims=True)
    spread = jnp.mean(centre * centre, axis=-1, keepdims=True)
    scale = lax.rsqrt(spread + EPSILON)
    return centre * scale, scale


def norm_back(grad, gain, hat, scale):
    e = grad * gain
    return scale * (
        e - jnp.mean(e, axis=-1, keepdims=True) - hat * jnp.mean(e * hat, axis=-1, keepdims=True)
    )


def branch_kernel(count, *refs):
    att_refs, weight_refs = refs[:count], refs[count : 2 * count]
    token_ref, bias_ref, gain_ref, shift_ref, middle_ref, h2_ref = refs[2 * count :]
    branch = bias_ref[...]
    for att, weight in zip(att_refs, weight_refs, strict=True):
        branch = branch + nn(att[...].T, weight[...])
    middle = token_ref[...].astype(F32) + branch
    middle_ref[...] = middle
    hat, _ = normalised(middle)
    h2_ref[...] = (hat * gain_ref[...] + shift_ref[...]).astype(BF)


def hidden_kernel(count, chunk, *refs):
    h2_refs, grad_refs = refs[:count], refs[count : 2 * count]
    fc_ref, proj_ref, bias_ref = refs[2 * count : 2 * count + 3]
    rest = refs[2 * count + 3 :]
    back_refs, act_refs, pre_refs, sum_ref = rest[:count], rest[count : 2 * count], rest[2 * count : 3 * count], rest[3 * count]
    sum_ref[...] = jnp.zeros_like(sum_ref)
    for r in range(count):

        def step(i, carry, r=r):
            at = rows_at(i, chunk)
            u = nn(h2_refs[r][at, :], fc_ref[...]) + bias_ref[...]
            grad_act = nn(grad_refs[r][at, :], proj_ref[...])
            square = u * u
            bend = jnp.tanh(GELU_SCALE * (u + 0.044715 * square * u))
            act_refs[r][at, :] = (0.5 * u * (1.0 + bend)).astype(BF)
            slope = 0.5 * (1.0 + bend) + 0.5 * u * (1.0 - bend * bend) * GELU_SCALE * (
                1.0 + 3.0 * 0.044715 * square
            )
            grad_pre = (grad_act * slope).astype(BF)
            pre_refs[r][at, :] = grad_pre
            sum_ref[...] += jnp.sum(grad_pre.astype(F32), axis=0, keepdims=True)
            back_refs[r][at, :] = nt(grad_pre, fc_ref[...]).astype(BF)
            return carry

        lax.fori_loop(0, h2_refs[r].shape[0] // chunk, step, 0)


def hidden(h2s, grads, fc, proj, bias):
    count = len(h2s)
    rows, width = h2s[0].shape
    cols = fc.shape[1]
    return kernel_call(
        functools.partial(hidden_kernel, count, 256),
        "hidden",
        [shape((rows, width), BF)] * count
        + [shape((rows, cols), BF)] * (2 * count)
        + [shape((1, cols), F32)],
        [],
        [*h2s, *grads, fc, proj, bias],
        6 * count * rows * width * cols,
        transcendentals=count * rows * cols,
    )


def split_store(value, keep_ref, give_ref, high, lanes):
    pairs, rows, _ = keep_ref.shape
    for p in range(pairs):
        lower = value[2 * p * rows : (2 * p + 1) * rows, :]
        upper = value[(2 * p + 1) * rows : (2 * p + 2) * rows, :]
        keep_ref[p, :, lanes] = jnp.where(high, upper, lower)
        give_ref[p, :, lanes] = jnp.where(high, lower, upper).astype(BF)


def weight_kernel(count, high_ref, *refs):
    left_refs, right_refs = refs[:count], refs[count : 2 * count]
    keep_ref, give_ref = refs[2 * count :]
    total = tn(left_refs[0][...], right_refs[0][...])
    for r in range(1, count):
        total = total + tn(left_refs[r][...], right_refs[r][...])
    split_store(total, keep_ref, give_ref, high_ref[0] > 0, slice(0, total.shape[1]))


def hidden_weights(lefts, rights, high, dp_size):
    rows, width = lefts[0].shape
    cols = rights[0].shape[1]
    dims = (dp_size // 2, width // dp_size, cols)
    return kernel_call(
        functools.partial(weight_kernel, len(lefts)),
        "hidden_weights",
        [shape(dims, F32), shape(dims, BF)],
        [high],
        [*lefts, *rights],
        2 * len(lefts) * rows * width * cols,
    )


def project_kernel(count, *refs):
    act_refs, proj_ref, out_refs = refs[:count], refs[count], refs[count + 1 :]
    for act, out in zip(act_refs, out_refs, strict=True):
        out[...] = nt(act[...], proj_ref[...]).astype(BF)


def project(acts, proj):
    rows, cols = acts[0].shape
    width = proj.shape[0]
    return kernel_call(
        functools.partial(project_kernel, len(acts)),
        "project",
        [shape((rows, width), BF)] * len(acts),
        [],
        [*acts, proj],
        2 * len(acts) * rows * cols * width,
    )


def middle_kernel(count, middle_ref, live_grad_ref, own_ref, near_ref, far_ref, gain_ref, *refs):
    weight_refs = refs[:count]
    grad_ref, branch_ref, sums_ref = refs[count : count + 3]
    att_refs = refs[count + 3 :]
    hat, scale = normalised(middle_ref[...])
    grad = own_ref[...].astype(F32) + near_ref[...].astype(F32) + far_ref[...].astype(F32)
    here = live_grad_ref[...].astype(F32)
    total = here + norm_back(grad, gain_ref[...], hat, scale)
    grad_ref[...] = total
    branch = total.astype(BF)
    branch_ref[...] = branch
    sums_ref[0:1, :] = jnp.sum(branch.astype(F32), axis=0, keepdims=True)
    sums_ref[1:2, :] = jnp.sum(grad * hat, axis=0, keepdims=True)
    sums_ref[2:3, :] = jnp.sum(grad, axis=0, keepdims=True)
    sums_ref[3:4, :] = jnp.sum(here, axis=0, keepdims=True)
    for weight, att in zip(weight_refs, att_refs, strict=True):
        att[...] = nt(branch, weight[...]).T.astype(BF)


def out_weight_kernel(count, branch_ref, *refs):
    for att, out in zip(refs[:count], refs[count:], strict=True):
        out[...] = nn(att[...], branch_ref[...]).astype(BF)


def first_kernel(order_ref, hat_ref, weight_ref, part_ref, keep_ref, give_ref, sums_ref, bias_ref):
    count, rows = 2 * keep_ref.shape[0], keep_ref.shape[1]
    sums_ref[...] = jnp.zeros_like(sums_ref)
    bias_ref[...] = jnp.zeros_like(bias_ref)

    def block(r):
        at = rows_at(order_ref[r], rows)
        part = part_ref[at, :]
        bias_ref[...] += jnp.sum(part.astype(F32), axis=0, keepdims=True)
        total = nt(part, weight_ref[...])
        sums_ref[0:1, :] += jnp.sum(total * hat_ref[at, :].astype(F32), axis=0, keepdims=True)
        sums_ref[1:2, :] += jnp.sum(total, axis=0, keepdims=True)
        return total.astype(BF)

    def pair(p, carry):
        give_ref[p] = block(2 * p + 1)
        keep_ref[p] = block(2 * p)
        return carry

    lax.fori_loop(0, count // 2, pair, 0)


def qkv_weight_kernel(count, high_ref, h1_ref, part_ref, *refs):
    out_refs = refs[:count]
    keep_ref, give_ref = refs[count:]
    high = high_ref[0] > 0
    cols = part_ref.shape[1]
    split_store(tn(h1_ref[...], part_ref[...]), keep_ref, give_ref, high, slice(0, cols))
    total = out_refs[0][...].astype(F32).T
    split_store(total, keep_ref, give_ref, high, slice(cols, cols + total.shape[1]))


def qkv_weights(h1, part, outs, high, dp_size):
    total, width = h1.shape
    dims = (dp_size // 2, width // dp_size, part.shape[1] + outs[0].shape[0])
    return kernel_call(
        functools.partial(qkv_weight_kernel, len(outs)),
        "qkv_weights",
        [shape(dims, F32), shape(dims, BF)],
        [high],
        [h1, part, *outs],
        2 * total * width * part.shape[1],
    )


def halve_kernel(high_ref, keep_ref, got_ref, keep_out, give_out):
    high = high_ref[0] > 0
    for p in range(keep_out.shape[0]):
        lower = keep_ref[2 * p] + got_ref[2 * p].astype(F32)
        upper = keep_ref[2 * p + 1] + got_ref[2 * p + 1].astype(F32)
        keep_out[p] = jnp.where(high, upper, lower)
        give_out[p] = jnp.where(high, lower, upper).astype(BF)


def halve(keep, got, axis, bit):
    dims = (keep.shape[0] // 2, *keep.shape[1:])
    high = jnp.reshape((lax.axis_index(axis) & bit) // bit, (1,)).astype(jnp.int32)
    return kernel_call(
        halve_kernel,
        "halve",
        [shape(dims, F32), shape(dims, BF)],
        [high],
        [keep, got],
        3 * keep.size,
    )


def token_kernel(token_ref, gain_ref, own_ref, near_ref, far_ref, middle_ref, out_ref):
    hat, scale = normalised(token_ref[...].astype(F32))
    grad = own_ref[...].astype(F32) + near_ref[...].astype(F32) + far_ref[...].astype(F32)
    out_ref[...] = (middle_ref[...] + norm_back(grad, gain_ref[...], hat, scale)).astype(BF)


def per_device(
    tokens,
    seq_lengths,
    norm1_gain,
    norm1_shift,
    qkv_weight,
    qv_bias,
    out_weight,
    out_bias,
    norm2_gain,
    norm2_shift,
    fc_weight,
    fc_bias,
    proj_weight,
    proj_bias,
    out_grad,
):
    tensor_size = lax.axis_size("tensor")
    assert tensor_size == 4
    near, far = 1, 2
    dp_size = lax.axis_size("dp")
    tensor_pos = lax.axis_index("tensor")
    local_rows, model_width = tokens.shape
    capacity = local_rows * tensor_size
    shard_rows = qkv_weight.shape[0]
    head_cols = qkv_weight.shape[2]
    heads = head_cols // HS
    hidden_cols = fc_weight.shape[1]
    high = jnp.reshape(lax.axis_index("dp") & 1, (1,)).astype(jnp.int32)

    def row(vector):
        return vector.reshape(1, -1)

    qkv_heads = qkv_weight.reshape(shard_rows, 3, heads, HS).transpose(0, 2, 1, 3)
    ahead = jnp.concatenate([qkv_heads.reshape(shard_rows, -1), out_weight.T], 1)[None]
    later = jnp.concatenate([fc_weight, proj_weight.T], 1)[None]
    far_tokens = swap(tokens, "tensor", far)
    dp_bits = bits_of("dp")[::-1]
    for k, bit in enumerate(dp_bits):
        if k == len(dp_bits) - 1:
            ahead = after(ahead, far_tokens)
        ahead = gather_step(ahead, "dp", bit)
        if k == len(dp_bits) - 2:
            for early in dp_bits[:-2]:
                later = gather_step(after(later, ahead), "dp", early)
    ahead = ahead.reshape(model_width, -1)
    later_far = swap(after(later, ahead), "dp", dp_bits[-2])
    full_qkv = ahead[:, : 3 * head_cols]
    out_turned = ahead[:, 3 * head_cols :].T
    outs = exchange([out_turned] * tensor_size, "tensor")
    near_tokens = swap(tokens, "tensor", near)
    last_tokens = swap(far_tokens, "tensor", near)
    token_blocks = [tokens, near_tokens, far_tokens, last_tokens]

    seg = segment_ids(seq_lengths, capacity)[0]
    live_here = lax.dynamic_slice_in_dim(seg, tensor_pos * local_rows, local_rows, 0) >= 0
    low = first_keys(seg, seq_lengths.shape[1])
    starts = low.reshape(tensor_size, local_rows)[:, 0] // local_rows
    order = jnp.concatenate(
        [
            lax.bitwise_xor(jnp.arange(tensor_size, dtype=jnp.int32), tensor_pos),
            jnp.reshape(tensor_pos, (1,)).astype(jnp.int32),
        ]
    )
    low = low.reshape(1, capacity)
    grad_mlp = jnp.where(live_here[:, None], out_grad, jnp.zeros_like(out_grad))
    far_grad = swap(after(grad_mlp, far_tokens), "tensor", far)
    near_grad = swap(grad_mlp, "tensor", near)
    token_blocks = after(tuple(token_blocks), far_grad)

    bias_here = lax.dynamic_slice_in_dim(qv_bias, tensor_pos * head_cols, head_cols, 1).reshape(
        2, heads, HS
    )
    bias_row = row(
        jnp.stack([bias_here[0], jnp.zeros((heads, HS), F32), bias_here[1]], 1).reshape(-1)
    )
    first_all, first_hat, queries, key_rows, values, attended, log_total, sends = attention_forward(
        token_blocks,
        full_qkv,
        bias_row,
        row(norm1_gain),
        row(norm1_shift),
        low,
        starts,
        order,
        heads,
    )

    outs = list(after(tuple(outs), sends))
    sends = after(sends, *outs)
    mine = exchange([sends[r] for r in range(tensor_size)], "tensor")
    later = gather_step(later, "dp", dp_bits[-2], after(later_far, sends))
    later = gather_step(later, "dp", dp_bits[-1]).reshape(model_width, -1)
    fc_cols, proj_turned = later[:, :hidden_cols], later[:, hidden_cols:]
    last_grad = swap(after(far_grad, sends), "tensor", near)
    grads = [grad_mlp, near_grad, far_grad, last_grad]
    middle, second_norm = kernel_call(
        functools.partial(branch_kernel, tensor_size),
        "branch",
        [shape((local_rows, model_width), F32), shape((local_rows, model_width), BF)],
        [],
        [*mine, *outs, tokens, row(out_bias), row(norm2_gain), row(norm2_shift)],
        2 * local_rows * model_width * model_width,
    )
    far_second = swap(second_norm, "tensor", far)
    near_second = swap(second_norm, "tensor", near)
    fc_bias_here = row(lax.dynamic_slice_in_dim(fc_bias, tensor_pos * hidden_cols, hidden_cols, 0))
    back_0, back_1, act_0, act_1, pre_0, pre_1, sum_pre_a = hidden(
        [second_norm, near_second], grads[:2], fc_cols, proj_turned, fc_bias_here
    )
    far_second = after(far_second, back_0)
    last_second = swap(far_second, "tensor", near)
    back_2, back_3, act_2, act_3, pre_2, pre_3, sum_pre_b = hidden(
        [far_second, last_second], grads[2:], fc_cols, proj_turned, fc_bias_here
    )
    near_back = swap(back_1, "tensor", near)
    last_back = swap(back_3, "tensor", near)
    chip_back = (back_2.astype(F32) + last_back.astype(F32)).astype(BF)
    far_back = swap(chip_back, "tensor", far)
    act_0, act_1, act_2, act_3, _ = lax.optimization_barrier((act_0, act_1, act_2, act_3, chip_back))
    acts = [act_0, act_1, act_2, act_3]
    pres = [pre_0, pre_1, pre_2, pre_3]
    keep_fc, give_fc = hidden_weights(
        [second_norm, near_second, far_second, last_second], pres, high, dp_size
    )
    got_fc = swap(give_fc, "dp", dp_bits[-1])
    keep_proj, give_proj = hidden_weights(
        [after(grads[0], keep_fc), *grads[1:]], acts, high, dp_size
    )
    got_proj = swap(give_proj, "dp", dp_bits[-1])
    mlp_parts = project(acts, after(proj_turned, keep_proj))
    mlp_near = swap(mlp_parts[1], "tensor", near)
    mlp_last = swap(mlp_parts[3], "tensor", near)
    mlp_far_sum = (mlp_parts[2].astype(F32) + mlp_last.astype(F32)).astype(BF)

    grad_middle, grad_branch, middle_sums, *grad_mine = kernel_call(
        functools.partial(middle_kernel, tensor_size),
        "middle",
        [
            shape((local_rows, model_width), F32),
            shape((local_rows, model_width), BF),
            shape((4, model_width), F32),
        ]
        + [shape((head_cols, local_rows), BF)] * tensor_size,
        [],
        [middle, grad_mlp, back_0, near_back, after(far_back, mlp_parts[0]), row(norm2_gain), *outs],
        2 * local_rows * model_width * model_width,
    )
    grad_attended = exchange(grad_mine, "tensor")
    mlp_far = swap(after(mlp_far_sum, grad_middle), "tensor", far)
    grad_out_parts = kernel_call(
        functools.partial(out_weight_kernel, tensor_size),
        "out_weights",
        [shape((head_cols, model_width), BF)] * tensor_size,
        [],
        [grad_branch, *mine],
        2 * local_rows * model_width * model_width,
    )
    keep_fc, give_fc = halve(keep_fc, after(got_fc, grad_out_parts[0]), "dp", dp_bits[-2])
    got_fc = swap(give_fc, "dp", dp_bits[-2])
    grad_out_parts = exchange(grad_out_parts, "tensor")
    (grad_qkv,) = attention_backward(
        0,
        heads,
        queries,
        key_rows,
        values,
        attended,
        log_total,
        grad_attended,
        after(low, keep_fc),
        starts,
        order,
    )
    grad_out_parts = after(tuple(grad_out_parts), grad_qkv)
    grad_out = sum(g.astype(F32) for g in grad_out_parts).astype(BF)
    grad_qkv = after(grad_qkv, grad_out)

    keep_first, give_first, first_sums, bias_sums = kernel_call(
        first_kernel,
        "first",
        [
            shape((tensor_size // 2, local_rows, model_width), BF),
            shape((tensor_size // 2, local_rows, model_width), BF),
            shape((2, model_width), F32),
            shape((1, 3 * head_cols), F32),
        ],
        [order],
        [first_hat, full_qkv, grad_qkv],
        2 * capacity * model_width * 3 * head_cols,
    )
    got_first = swap(give_first, "tensor", near)
    rest = dp_bits[:-2][::-1]
    got_fc = after(got_fc, keep_first)
    got_proj = after(got_proj, keep_first)
    for bit in rest:
        keep_fc, give_fc = halve(keep_fc, got_fc, "dp", bit)
        got_fc = swap(give_fc, "dp", bit)
    keep_proj, give_proj = halve(keep_proj, got_proj, "dp", dp_bits[-2])
    got_proj = swap(give_proj, "dp", dp_bits[-2])
    keep_qkv, give_qkv = qkv_weights(
        after(first_all, keep_fc, keep_proj), grad_qkv, [grad_out], high, dp_size
    )
    got_qkv = swap(give_qkv, "dp", dp_bits[-1])
    got_first = after(got_first, keep_qkv)
    chip_first = (keep_first[1].astype(F32) + got_first[1].astype(F32)).astype(BF)
    far_first = swap(chip_first, "tensor", far)
    got_proj = after(got_proj, chip_first)
    for bit in rest:
        keep_proj, give_proj = halve(keep_proj, got_proj, "dp", bit)
        got_proj = swap(give_proj, "dp", bit)
    mlp_out = mlp_parts[0].astype(F32) + mlp_near.astype(F32) + mlp_far.astype(F32)
    result = jnp.where(
        after(live_here, keep_proj)[:, None], middle + mlp_out + proj_bias, 0.0
    ).astype(BF)
    got_qkv = after(got_qkv, result)
    for k, bit in enumerate(dp_bits[:-1][::-1]):
        keep_qkv, give_qkv = halve(keep_qkv, got_qkv, "dp", bit)
        got_qkv = swap(give_qkv, "dp", bit)
        if k == 0:
            sum_fc = keep_fc[0] + after(got_fc, keep_qkv)[0].astype(F32)
            sum_proj = (keep_proj[0] + after(got_proj, keep_qkv)[0].astype(F32)).T
    far_first = after(far_first, keep_qkv)
    (grad_tokens,) = kernel_call(
        token_kernel,
        "token_gradient",
        [shape((local_rows, model_width), BF)],
        [],
        [tokens, row(norm1_gain), keep_first[0], got_first[0], far_first, grad_middle],
        0,
    )

    sum_qkv = keep_qkv[0] + after(got_qkv, grad_tokens)[0].astype(F32)
    sum_out = sum_qkv[:, 3 * head_cols :].T
    sum_qkv = (
        sum_qkv[:, : 3 * head_cols]
        .reshape(shard_rows, heads, 3, HS)
        .transpose(0, 2, 1, 3)
        .reshape(shard_rows, 3, head_cols)
    )
    bias_sums = bias_sums.reshape(heads, 3, HS)[:, 0::2].transpose(1, 0, 2).reshape(2, head_cols)
    qv_full = lax.dynamic_update_slice_in_dim(
        jnp.zeros((2, model_width), F32), bias_sums, tensor_pos * head_cols, 1
    )
    fc_full = lax.dynamic_update_slice_in_dim(
        jnp.zeros(fc_bias.shape, F32),
        (sum_pre_a + sum_pre_b).reshape(-1),
        tensor_pos * hidden_cols,
        0,
    )
    small = everyone_sum(
        jnp.concatenate(
            [after(first_sums, chip_first).reshape(-1), qv_full.reshape(-1), middle_sums.reshape(-1), fc_full]
        ).reshape(-1, 128),
        ("tensor", "dp"),
    ).reshape(-1)
    w = model_width
    return (
        result,
        grad_tokens,
        small[:w],
        small[w : 2 * w],
        sum_qkv,
        small[2 * w : 4 * w].reshape(2, w),
        sum_out,
        small[4 * w : 5 * w],
        small[5 * w : 6 * w],
        small[6 * w : 7 * w],
        sum_fc,
        small[8 * w :],
        sum_proj,
        small[7 * w : 8 * w],
    )


def solution(mesh):
    placed = (
        P(("dp", "tensor"), None),
        P("dp", None),
        P(),
        P(),
        P("dp", None, "tensor"),
        P(),
        P("tensor", "dp"),
        P(),
        P(),
        P(),
        P("dp", "tensor"),
        P(),
        P("tensor", "dp"),
        P(),
        P(("dp", "tensor"), None),
    )
    return jax.shard_map(
        per_device,
        mesh=mesh,
        in_specs=placed,
        out_specs=(
            P(("dp", "tensor"), None),
            P(("dp", "tensor"), None),
            P(),
            P(),
            P("dp", None, "tensor"),
            P(),
            P("tensor", "dp"),
            P(),
            P(),
            P(),
            P("dp", "tensor"),
            P(),
            P("tensor", "dp"),
            P(),
        ),
        check_vma=False,
    )
```

```python
import functools

import jax
import jax.numpy as jnp
from jax import lax
from jax.experimental import pallas as pl
from jax.experimental.pallas import tpu as pltpu
from jax.sharding import PartitionSpec as P

HS = 64
BLK = 128


EPSILON = 1e-05
MASKED = -1e30
GELU_SCALE = 0.7978845608028654

BF = jnp.bfloat16
F32 = jnp.float32


def segment_ids(lengths, capacity):
    padded = (lengths + BLK - 1) // BLK * BLK
    starts = jnp.cumsum(padded, axis=1) - padded
    places = jnp.arange(capacity, dtype=jnp.int32)
    inside = (places[None, None, :] >= starts[:, :, None]) & (
        places[None, None, :] < (starts + lengths)[:, :, None]
    )
    labels = jnp.arange(lengths.shape[1], dtype=jnp.int32)[None, :, None] + 1
    return jnp.sum(jnp.where(inside, labels, 0), axis=1) - 1


def swap(value, axis, bits):
    size = lax.axis_size(axis)
    return lax.ppermute(value, axis, [(i, i ^ bits) for i in range(size)])


def bits_of(axis):
    size = lax.axis_size(axis)
    count = size.bit_length() - 1
    assert 1 << count == size
    return [1 << b for b in range(count)]


def after(value, *others):
    return lax.optimization_barrier((value, *others))[0]


def gather_step(full, axis, bit, other=None):
    high = (lax.axis_index(axis) & bit) > 0
    other = swap(full, axis, bit) if other is None else other
    return jnp.where(
        high, jnp.stack([other, full], 1), jnp.stack([full, other], 1)
    ).reshape(-1, *full.shape[1:])


def exchange(blocks, axis):
    return [b if r == 0 else swap(b, axis, r) for r, b in enumerate(blocks)]


def everyone_sum(value, axes):
    for axis in axes:
        for bit in bits_of(axis):
            value = value + swap(value, axis, bit)
    return value


def first_keys(seg, slots):
    places = jnp.arange(seg.shape[0], dtype=jnp.int32)
    begins = jnp.where(seg != jnp.concatenate([jnp.full((1,), -2, jnp.int32), seg[:-1]]), places, 0)
    labels = jnp.arange(slots, dtype=jnp.int32)
    starts = jnp.sum(jnp.where((seg[None] == labels[:, None]), begins[None], 0), axis=1)
    mine = jnp.sum(jnp.where(seg[:, None] == labels[None], starts[None], 0), axis=1)
    return jnp.where(seg >= 0, mine, places)


def nt(a, b):
    return lax.dot_general(a, b, (((1,), (1,)), ((), ())), preferred_element_type=F32)


def nn(a, b):
    return lax.dot_general(a, b, (((1,), (0,)), ((), ())), preferred_element_type=F32)


def tn(a, b):
    return lax.dot_general(a, b, (((0,), (0,)), ((), ())), preferred_element_type=F32)


def rows_at(block, size):
    return pl.ds(pl.multiple_of(block * size, size), size)


def masked_scores(keys, queries, low, first_key, first_query):
    scores = nt(keys, queries)
    key_at = lax.broadcasted_iota(jnp.int32, scores.shape, 0) + first_key
    query_at = lax.broadcasted_iota(jnp.int32, (1, scores.shape[1]), 1) + first_query
    return jnp.where((key_at >= low) & (key_at <= query_at), scores, MASKED)


def forward_kernel(heads, block, here_ref, start_ref, low_ref, *refs):
    count = here_ref.shape[0] - 1
    token_refs = refs[:count]
    weight_ref, bias_ref, gain_ref, shift_ref = refs[count : count + 4]
    h1_ref, hat_ref, q_ref, k_ref, v_ref, out_ref, lse_ref = refs[count + 4 : count + 11]
    send_refs, token_all = refs[count + 11 : -1], refs[-1]
    here = here_ref[count]
    local_rows = token_refs[0].shape[0]
    chunk = 256
    for r in range(count):
        token_all[r] = token_refs[r][...]
    if True:

        def project(step, carry):
            r, part = step // (local_rows // chunk), step % (local_rows // chunk)
            base = pl.multiple_of(here_ref[r] * local_rows + part * chunk, chunk)
            rows = token_all[r, rows_at(part, chunk), :].astype(F32)
            centre = rows - jnp.mean(rows, axis=-1, keepdims=True)
            spread = jnp.mean(centre * centre, axis=-1, keepdims=True)
            hat = centre * lax.rsqrt(spread + EPSILON)
            h1 = (hat * gain_ref[...] + shift_ref[...]).astype(BF)
            hat_ref[pl.ds(base, chunk), :] = hat.astype(BF)
            h1_ref[pl.ds(base, chunk), :] = h1
            qkv = (nn(h1, weight_ref[:, : 3 * heads * HS]) + bias_ref[...]).astype(BF)
            for h in range(heads):
                at = 3 * h * HS
                q_ref[h, pl.ds(base, chunk), :] = qkv[:, at : at + HS] * HS ** (-0.5)
                k_ref[h, pl.ds(base, chunk), :] = qkv[:, at + HS : at + 2 * HS]
                v_ref[h, pl.ds(base, chunk), :] = qkv[:, at + 2 * HS : at + 3 * HS]
            return carry

        lax.fori_loop(0, count * local_rows // chunk, project, 0)

    blocks = q_ref.shape[1] // block

    def query_step(i, carry):
        low = low_ref[0:1, rows_at(i, block)]

        def key_step(j, state):
            fresh = []
            for h in range(heads):
                peak, total, acc = state[3 * h : 3 * h + 3]
                scores = masked_scores(
                    k_ref[h, rows_at(j, block), :],
                    q_ref[h, rows_at(i, block), :],
                    low,
                    j * block,
                    i * block,
                )
                peak_now = jnp.maximum(peak, jnp.max(scores, axis=0, keepdims=True))
                decay = jnp.exp(peak - peak_now)
                weights = jnp.exp(scores - peak_now)
                total = total * decay + jnp.sum(weights, axis=0, keepdims=True)
                acc = acc * decay + tn(v_ref[h, rows_at(j, block), :], weights.astype(BF))
                fresh += [peak_now, total, acc]
            return tuple(fresh)

        init = (
            jnp.full((1, block), MASKED, F32),
            jnp.zeros((1, block), F32),
            jnp.zeros((HS, block), F32),
        ) * heads
        state = lax.fori_loop(start_ref[i], i + 1, key_step, init)
        slot = lax.bitwise_xor(i, here)
        for h in range(heads):
            peak, total, acc = state[3 * h : 3 * h + 3]
            rows = acc / total
            out_ref[h, :, rows_at(i, block)] = rows
            lse_ref[h, :, rows_at(i, block)] = peak + jnp.log(total)
            for r in range(count):

                @pl.when(slot == r)
                def _(r=r, h=h, rows=rows):
                    send_refs[r][h * HS : (h + 1) * HS, :] = rows.astype(BF)

        return carry

    lax.fori_loop(0, blocks, query_step, 0)


def attention_forward(blocks, weight, bias, gain, shift, low, starts, order, heads):
    rows, width = blocks[0].shape
    count = len(blocks)
    total = rows * count
    flops = 2 * total * width * weight.shape[1] + 2 * heads * total * total * HS
    return pl.pallas_call(
        functools.partial(forward_kernel, heads, rows),
        out_shape=(
            shape((total, width), BF),
            shape((total, width), BF),
            shape((heads, total, HS), BF),
            shape((heads, total, HS), BF),
            shape((heads, total, HS), BF),
            shape((heads, HS, total), F32),
            shape((heads, 1, total), F32),
        )
        + (shape((heads * HS, rows), BF),) * count,
        in_specs=[pl.BlockSpec(memory_space=pltpu.SMEM)] * 2
        + [pl.BlockSpec(memory_space=pltpu.VMEM)] * (count + 5),
        out_specs=[pl.BlockSpec(memory_space=pltpu.VMEM)] * (7 + count),
        scratch_shapes=[pltpu.VMEM((count, rows, width), BF)],
        compiler_params=pltpu.CompilerParams(vmem_limit_bytes=60000 * 1024),
        cost_estimate=pl.CostEstimate(
            flops=flops, bytes_accessed=24 << 20, transcendentals=heads * total * total // 2
        ),
        name="attention_forward",
    )(order, starts, low, *blocks, weight, bias, gain, shift)


def backward_kernel(
    first_head, heads, block, start_ref, order_ref, low_ref, q_ref, k_ref, v_ref, out_ref, lse_ref, *refs
):
    count = order_ref.shape[0] - 1
    grad_refs = refs[:count]
    result_ref = refs[count]
    grad_t_ref, grad_ref, centre_ref, dk_ref, dv_ref, kt_ref, dq_ref = refs[count + 1 :]
    for r in range(count):
        for h in range(heads):
            whole = first_head + h
            piece = grad_refs[r][whole * HS : (whole + 1) * HS, :]
            at = rows_at(order_ref[r], block)
            grad_t_ref[h, :, at] = piece
            grad_ref[h, at, :] = piece.T
            centre_ref[h, :, at] = jnp.sum(
                piece.astype(F32) * out_ref[whole, :, at], axis=0, keepdims=True
            )
            kt_ref[h, :, r * block : (r + 1) * block] = k_ref[
                whole, r * block : (r + 1) * block, :
            ].T
    dk_ref[...] = jnp.zeros_like(dk_ref)
    dv_ref[...] = jnp.zeros_like(dv_ref)
    blocks = q_ref.shape[1] // block

    def query_step(i, carry):
        here = rows_at(i, block)
        low = low_ref[0:1, here]

        def key_step(j, state):
            there = rows_at(j, block)
            fresh = []
            for h in range(heads):
                whole = first_head + h
                queries = q_ref[whole, here, :]
                scores = masked_scores(k_ref[whole, there, :], queries, low, j * block, i * block)
                probs = jnp.exp(scores - lse_ref[whole, :, here])
                grad_probs = nn(v_ref[whole, there, :], grad_t_ref[h, :, here])
                grad_scores = (probs * (grad_probs - centre_ref[h, :, here])).astype(BF)
                dv_ref[h, there, :] += nn(probs.astype(BF), grad_ref[h, here, :])
                dk_ref[h, there, :] += nn(grad_scores, queries)
                fresh.append(state[h] + nn(kt_ref[h, :, there], grad_scores))
            return tuple(fresh)

        state = lax.fori_loop(
            start_ref[i], i + 1, key_step, (jnp.zeros((HS, block), F32),) * heads
        )
        for h in range(heads):
            dq_ref[h, here, :] = (state[h] * HS ** (-0.5)).T.astype(BF)
        return carry

    lax.fori_loop(0, blocks, query_step, 0)

    def finish(i, carry):
        here = rows_at(i, block)
        pieces = []
        for h in range(heads):
            pieces += [dq_ref[h, here, :], dk_ref[h, here, :].astype(BF), dv_ref[h, here, :].astype(BF)]
        result_ref[here, :] = jnp.concatenate(pieces, axis=1)
        return carry

    lax.fori_loop(0, blocks, finish, 0)


def vmem(count):
    return [pl.BlockSpec(memory_space=pltpu.VMEM)] * count


def smem(count):
    return [pl.BlockSpec(memory_space=pltpu.SMEM)] * count


def kernel_call(body, name, out_shape, scalars, arrays, flops, scratch=(), transcendentals=0):
    moved = sum(a.size * a.dtype.itemsize for a in arrays) + sum(
        o.size * jnp.dtype(o.dtype).itemsize for o in out_shape
    )
    return pl.pallas_call(
        body,
        out_shape=tuple(out_shape),
        in_specs=smem(len(scalars)) + vmem(len(arrays)),
        out_specs=vmem(len(out_shape)),
        scratch_shapes=list(scratch),
        compiler_params=pltpu.CompilerParams(vmem_limit_bytes=60000 * 1024),
        cost_estimate=pl.CostEstimate(
            flops=flops, bytes_accessed=moved, transcendentals=transcendentals
        ),
        name=name,
    )(*scalars, *arrays)


def shape(dims, kind):
    return jax.ShapeDtypeStruct(dims, kind)


def attention_backward(first_head, heads, q, k, v, out, lse, grads, low, starts, order):
    total = q.shape[1]
    rows = total // len(grads)
    return kernel_call(
        functools.partial(backward_kernel, first_head, heads, rows),
        "attention_backward",
        [shape((total, 3 * HS * heads), BF)],
        [starts, order],
        [low, q, k, v, out, lse, *grads],
        5 * heads * total * total * HS,
        [
            pltpu.VMEM((heads, HS, total), BF),
            pltpu.VMEM((heads, total, HS), BF),
            pltpu.VMEM((heads, 1, total), F32),
            pltpu.VMEM((heads, total, HS), F32),
            pltpu.VMEM((heads, total, HS), F32),
            pltpu.VMEM((heads, HS, total), BF),
            pltpu.VMEM((heads, total, HS), BF),
        ],
        heads * total * total // 2,
    )


def normalised(rows):
    centre = rows - jnp.mean(rows, axis=-1, keepdims=True)
    spread = jnp.mean(centre * centre, axis=-1, keepdims=True)
    scale = lax.rsqrt(spread + EPSILON)
    return centre * scale, scale


def norm_back(grad, gain, hat, scale):
    e = grad * gain
    return scale * (
        e - jnp.mean(e, axis=-1, keepdims=True) - hat * jnp.mean(e * hat, axis=-1, keepdims=True)
    )


def turn_kernel(packed_ref, out_ref):
    out_ref[...] = packed_ref[:, packed_ref.shape[1] - out_ref.shape[0] :].T


def branch_kernel(count, *refs):
    att_refs, weight_refs = refs[:count], refs[count : 2 * count]
    token_ref, bias_ref, gain_ref, shift_ref, middle_ref, h2_ref = refs[2 * count :]
    branch = bias_ref[...]
    for att, weight in zip(att_refs, weight_refs, strict=True):
        branch = branch + nn(att[...].T, weight[...])
    middle = token_ref[...].astype(F32) + branch
    middle_ref[...] = middle
    hat, _ = normalised(middle)
    h2_ref[...] = (hat * gain_ref[...] + shift_ref[...]).astype(BF)


def hidden_kernel(count, chunk, *refs):
    h2_refs, grad_refs = refs[:count], refs[count : 2 * count]
    packed_ref, bias_ref = refs[2 * count : 2 * count + 2]
    back_refs = refs[2 * count + 2 : 3 * count + 2]
    act_ref, pre_ref, sum_ref, h2_all, grad_all = refs[3 * count + 2 :]
    rows, cols = h2_refs[0].shape[0], packed_ref.shape[1] // 2
    fc_ref, proj_ref = packed_ref.at[:, :cols], packed_ref.at[:, cols:]
    sum_ref[...] = jnp.zeros_like(sum_ref)
    for r in range(count):
        h2_all[r] = h2_refs[r][...]
        grad_all[r] = grad_refs[r][...]

    def step(i, carry):
        r = i // (rows // chunk)
        at = rows_at(i % (rows // chunk), chunk)
        u = nn(h2_all[r, at, :], fc_ref[...]) + bias_ref[...]
        grad_act = nn(grad_all[r, at, :], proj_ref[...])
        square = u * u
        bend = jnp.tanh(GELU_SCALE * (u + 0.044715 * square * u))
        act_ref[r, at, :] = (0.5 * u * (1.0 + bend)).astype(BF)
        slope = 0.5 * (1.0 + bend) + 0.5 * u * (1.0 - bend * bend) * GELU_SCALE * (
            1.0 + 3.0 * 0.044715 * square
        )
        grad_pre = (grad_act * slope).astype(BF)
        pre_ref[r, at, :] = grad_pre
        sum_ref[...] += jnp.sum(grad_pre.astype(F32), axis=0, keepdims=True)
        back = nt(grad_pre, fc_ref[...]).astype(BF)
        for k in range(count):

            @pl.when(r == k)
            def _(k=k, back=back, at=at):
                back_refs[k][at, :] = back

        return carry

    lax.fori_loop(0, count * rows // chunk, step, 0)


def hidden(h2s, grads, packed, bias):
    count = len(h2s)
    rows, width = h2s[0].shape
    cols = packed.shape[1] // 2
    return kernel_call(
        functools.partial(hidden_kernel, count, 256),
        "hidden",
        [shape((rows, width), BF)] * count
        + [shape((count, rows, cols), BF)] * 2
        + [shape((1, cols), F32)],
        [],
        [*h2s, *grads, packed, bias],
        6 * count * rows * width * cols,
        [pltpu.VMEM((count, rows, width), BF)] * 2,
        transcendentals=count * rows * cols,
    )


def split_store(value, keep_ref, give_ref, high, lanes):
    pairs, rows, _ = keep_ref.shape
    for p in range(pairs):
        lower = value[2 * p * rows : (2 * p + 1) * rows, :]
        upper = value[(2 * p + 1) * rows : (2 * p + 2) * rows, :]
        keep_ref[p, :, lanes] = jnp.where(high, upper, lower)
        give_ref[p, :, lanes] = jnp.where(high, lower, upper).astype(BF)


def weight_kernel(count, high_ref, *refs):
    left_refs, right_refs = refs[:count], refs[count:-2]
    keep_ref, give_ref = refs[-2:]
    each = count // len(right_refs)
    total = tn(left_refs[0][...], right_refs[0][0])
    for r in range(1, count):
        total = total + tn(left_refs[r][...], right_refs[r // each][r % each])
    split_store(total, keep_ref, give_ref, high_ref[0] > 0, slice(0, total.shape[1]))


def hidden_weights(lefts, rights, high, dp_size):
    rows, width = lefts[0].shape
    cols = rights[0].shape[2]
    dims = (dp_size // 2, width // dp_size, cols)
    return kernel_call(
        functools.partial(weight_kernel, len(lefts)),
        "hidden_weights",
        [shape(dims, F32), shape(dims, BF)],
        [high],
        [*lefts, *rights],
        2 * len(lefts) * rows * width * cols,
    )


def project_kernel(count, *refs):
    act_refs, proj_ref, out_refs = refs[: -count - 1], refs[-count - 1], refs[-count:]
    each = count // len(act_refs)
    for r, out in enumerate(out_refs):
        act = act_refs[r // each].at[r % each]
        out[...] = nt(act[...], proj_ref[:, act.shape[1] :]).astype(BF)


def project(acts, packed):
    each, rows, cols = acts[0].shape
    width = packed.shape[0]
    count = each * len(acts)
    return kernel_call(
        functools.partial(project_kernel, count),
        "project",
        [shape((rows, width), BF)] * count,
        [],
        [*acts, packed],
        2 * count * rows * cols * width,
    )


def middle_kernel(count, middle_ref, live_grad_ref, own_ref, near_ref, far_ref, gain_ref, *refs):
    weight_refs = refs[:count]
    grad_ref, branch_ref, sums_ref = refs[count : count + 3]
    att_refs = refs[count + 3 :]
    hat, scale = normalised(middle_ref[...])
    grad = own_ref[...].astype(F32) + near_ref[...].astype(F32) + far_ref[...].astype(F32)
    here = live_grad_ref[...].astype(F32)
    total = here + norm_back(grad, gain_ref[...], hat, scale)
    grad_ref[...] = total
    branch = total.astype(BF)
    branch_ref[...] = branch
    sums_ref[0:1, :] = jnp.sum(branch.astype(F32), axis=0, keepdims=True)
    sums_ref[1:2, :] = jnp.sum(grad * hat, axis=0, keepdims=True)
    sums_ref[2:3, :] = jnp.sum(grad, axis=0, keepdims=True)
    sums_ref[3:4, :] = jnp.sum(here, axis=0, keepdims=True)
    for weight, att in zip(weight_refs, att_refs, strict=True):
        att[...] = nt(branch, weight[...]).T.astype(BF)


def out_weight_kernel(count, branch_ref, *refs):
    for att, out in zip(refs[:count], refs[count:], strict=True):
        out[...] = nn(att[...], branch_ref[...]).astype(BF)


def first_kernel(
    order_ref, hat_ref, weight_ref, part_ref, own_ref, far_ref, give_ref, sums_ref, bias_ref
):
    rows, cols = own_ref.shape[0], part_ref.shape[1]
    sums_ref[...] = jnp.zeros_like(sums_ref)
    bias_ref[...] = jnp.zeros_like(bias_ref)

    def step(r, carry):
        at = rows_at(order_ref[r], rows)
        part = part_ref[at, :]
        bias_ref[...] += jnp.sum(part.astype(F32), axis=0, keepdims=True)
        total = nt(part, weight_ref[:, :cols])
        sums_ref[0:1, :] += jnp.sum(total * hat_ref[at, :].astype(F32), axis=0, keepdims=True)
        sums_ref[1:2, :] += jnp.sum(total, axis=0, keepdims=True)
        done = total.astype(BF)

        @pl.when(r == 0)
        def _():
            own_ref[...] = done

        @pl.when(r == 2)
        def _():
            far_ref[...] = done

        @pl.when((r & 1) == 1)
        def _():
            give_ref[r // 2] = done

        return carry

    lax.fori_loop(0, 4, step, 0)


def qkv_weight_kernel(count, high_ref, h1_ref, part_ref, *refs):
    out_refs = refs[:count]
    keep_ref, give_ref = refs[count:]
    high = high_ref[0] > 0
    cols = part_ref.shape[1]
    split_store(tn(h1_ref[...], part_ref[...]), keep_ref, give_ref, high, slice(0, cols))
    total = out_refs[0][...].astype(F32).T
    split_store(total, keep_ref, give_ref, high, slice(cols, cols + total.shape[1]))


def qkv_weights(h1, part, outs, high, dp_size):
    total, width = h1.shape
    dims = (dp_size // 2, width // dp_size, part.shape[1] + outs[0].shape[0])
    return kernel_call(
        functools.partial(qkv_weight_kernel, len(outs)),
        "qkv_weights",
        [shape(dims, F32), shape(dims, BF)],
        [high],
        [h1, part, *outs],
        2 * total * width * part.shape[1],
    )


def halve_kernel(high_ref, keep_ref, got_ref, keep_out, give_out):
    high = high_ref[0] > 0
    for p in range(keep_out.shape[0]):
        lower = keep_ref[2 * p] + got_ref[2 * p].astype(F32)
        upper = keep_ref[2 * p + 1] + got_ref[2 * p + 1].astype(F32)
        keep_out[p] = jnp.where(high, upper, lower)
        give_out[p] = jnp.where(high, lower, upper).astype(BF)


def halve(keep, got, axis, bit):
    dims = (keep.shape[0] // 2, *keep.shape[1:])
    high = jnp.reshape((lax.axis_index(axis) & bit) // bit, (1,)).astype(jnp.int32)
    return kernel_call(
        halve_kernel,
        "halve",
        [shape(dims, F32), shape(dims, BF)],
        [high],
        [keep, got],
        3 * keep.size,
    )


def token_kernel(token_ref, gain_ref, own_ref, near_ref, far_ref, middle_ref, out_ref):
    hat, scale = normalised(token_ref[...].astype(F32))
    grad = own_ref[...].astype(F32) + near_ref[0].astype(F32) + far_ref[...].astype(F32)
    out_ref[...] = (middle_ref[...] + norm_back(grad, gain_ref[...], hat, scale)).astype(BF)


def per_device(
    tokens,
    seq_lengths,
    norm1_gain,
    norm1_shift,
    qkv_weight,
    qv_bias,
    out_weight,
    out_bias,
    norm2_gain,
    norm2_shift,
    fc_weight,
    fc_bias,
    proj_weight,
    proj_bias,
    out_grad,
):
    tensor_size = lax.axis_size("tensor")
    assert tensor_size == 4
    near, far = 1, 2
    dp_size = lax.axis_size("dp")
    tensor_pos = lax.axis_index("tensor")
    local_rows, model_width = tokens.shape
    capacity = local_rows * tensor_size
    shard_rows = qkv_weight.shape[0]
    head_cols = qkv_weight.shape[2]
    heads = head_cols // HS
    hidden_cols = fc_weight.shape[1]
    high = jnp.reshape(lax.axis_index("dp") & 1, (1,)).astype(jnp.int32)

    def row(vector):
        return vector.reshape(1, -1)

    qkv_heads = qkv_weight.reshape(shard_rows, 3, heads, HS).transpose(0, 2, 1, 3)
    ahead = jnp.concatenate([qkv_heads.reshape(shard_rows, -1), out_weight.T], 1)[None]
    later = jnp.concatenate([fc_weight, proj_weight.T], 1)[None]
    far_tokens = swap(tokens, "tensor", far)
    dp_bits = bits_of("dp")[::-1]
    for k, bit in enumerate(dp_bits):
        if k == len(dp_bits) - 1:
            ahead = after(ahead, far_tokens)
        ahead = gather_step(ahead, "dp", bit)
        if k == len(dp_bits) - 2:
            for early in dp_bits[:-2]:
                later = gather_step(after(later, ahead), "dp", early)
    ahead = ahead.reshape(model_width, -1)
    later_far = swap(after(later, ahead), "dp", dp_bits[-2])
    full_qkv = ahead
    (out_turned,) = kernel_call(
        turn_kernel, "turn", [shape((head_cols, model_width), BF)], [], [ahead], 0
    )
    outs = exchange([out_turned] * tensor_size, "tensor")
    near_tokens = swap(tokens, "tensor", near)
    last_tokens = swap(far_tokens, "tensor", near)
    token_blocks = [tokens, near_tokens, far_tokens, last_tokens]

    seg = segment_ids(seq_lengths, capacity)[0]
    live_here = lax.dynamic_slice_in_dim(seg, tensor_pos * local_rows, local_rows, 0) >= 0
    low = first_keys(seg, seq_lengths.shape[1])
    starts = low.reshape(tensor_size, local_rows)[:, 0] // local_rows
    order = jnp.concatenate(
        [
            lax.bitwise_xor(jnp.arange(tensor_size, dtype=jnp.int32), tensor_pos),
            jnp.reshape(tensor_pos, (1,)).astype(jnp.int32),
        ]
    )
    low = low.reshape(1, capacity)
    grad_mlp = jnp.where(live_here[:, None], out_grad, jnp.zeros_like(out_grad))
    far_grad = swap(after(grad_mlp, far_tokens), "tensor", far)
    near_grad = swap(grad_mlp, "tensor", near)

    bias_here = lax.dynamic_slice_in_dim(qv_bias, tensor_pos * head_cols, head_cols, 1).reshape(
        2, heads, HS
    )
    bias_row = row(
        jnp.stack([bias_here[0], jnp.zeros((heads, HS), F32), bias_here[1]], 1).reshape(-1)
    )
    first_all, first_hat, queries, key_rows, values, attended, log_total, *sends = attention_forward(
        token_blocks,
        full_qkv,
        bias_row,
        row(norm1_gain),
        row(norm1_shift),
        low,
        starts,
        order,
        heads,
    )

    outs = list(after(tuple(outs), sends[0]))
    sends = after(tuple(sends), far_grad, *outs)
    mine = exchange(sends, "tensor")
    later = gather_step(later, "dp", dp_bits[-2], after(later_far, sends[0]))
    later = gather_step(later, "dp", dp_bits[-1]).reshape(model_width, -1)
    last_grad = swap(after(far_grad, sends[0]), "tensor", near)
    grads = [grad_mlp, near_grad, far_grad, last_grad]
    middle, second_norm = kernel_call(
        functools.partial(branch_kernel, tensor_size),
        "branch",
        [shape((local_rows, model_width), F32), shape((local_rows, model_width), BF)],
        [],
        [*mine, *outs, tokens, row(out_bias), row(norm2_gain), row(norm2_shift)],
        2 * local_rows * model_width * model_width,
    )
    far_second = swap(second_norm, "tensor", far)
    near_second = swap(second_norm, "tensor", near)
    fc_bias_here = row(lax.dynamic_slice_in_dim(fc_bias, tensor_pos * hidden_cols, hidden_cols, 0))
    back_0, back_1, act_a, pre_a, sum_pre_a = hidden(
        [second_norm, near_second], grads[:2], later, fc_bias_here
    )
    far_second = after(far_second, back_0)
    last_second = swap(far_second, "tensor", near)
    back_2, back_3, act_b, pre_b, sum_pre_b = hidden(
        [far_second, last_second], grads[2:], later, fc_bias_here
    )
    near_back = swap(back_1, "tensor", near)
    last_back = swap(back_3, "tensor", near)
    chip_back = (back_2.astype(F32) + last_back.astype(F32)).astype(BF)
    far_back = swap(chip_back, "tensor", far)
    act_a, act_b = after((act_a, act_b), chip_back)
    acts = [act_a, act_b]
    pres = [pre_a, pre_b]
    keep_fc, give_fc = hidden_weights(
        [second_norm, near_second, far_second, last_second], pres, high, dp_size
    )
    got_fc = swap(give_fc, "dp", dp_bits[-1])
    keep_proj, give_proj = hidden_weights(
        [after(grads[0], keep_fc), *grads[1:]], acts, high, dp_size
    )
    got_proj = swap(give_proj, "dp", dp_bits[-1])
    mlp_parts = project(acts, after(later, keep_proj))
    mlp_near = swap(mlp_parts[1], "tensor", near)
    mlp_last = swap(mlp_parts[3], "tensor", near)
    mlp_far_sum = (mlp_parts[2].astype(F32) + mlp_last.astype(F32)).astype(BF)

    grad_middle, grad_branch, middle_sums, *grad_mine = kernel_call(
        functools.partial(middle_kernel, tensor_size),
        "middle",
        [
            shape((local_rows, model_width), F32),
            shape((local_rows, model_width), BF),
            shape((4, model_width), F32),
        ]
        + [shape((head_cols, local_rows), BF)] * tensor_size,
        [],
        [middle, grad_mlp, back_0, near_back, after(far_back, mlp_parts[0]), row(norm2_gain), *outs],
        2 * local_rows * model_width * model_width,
    )
    grad_attended = exchange(grad_mine, "tensor")
    mlp_far = swap(after(mlp_far_sum, grad_middle), "tensor", far)
    grad_out_parts = kernel_call(
        functools.partial(out_weight_kernel, tensor_size),
        "out_weights",
        [shape((head_cols, model_width), BF)] * tensor_size,
        [],
        [after(grad_branch, mlp_far_sum), *mine],
        2 * local_rows * model_width * model_width,
    )
    keep_fc, give_fc = halve(keep_fc, after(got_fc, grad_out_parts[0]), "dp", dp_bits[-2])
    got_fc = swap(give_fc, "dp", dp_bits[-2])
    grad_out_parts = exchange(grad_out_parts, "tensor")
    (grad_qkv,) = attention_backward(
        0,
        heads,
        queries,
        key_rows,
        values,
        attended,
        log_total,
        grad_attended,
        after(low, keep_fc),
        starts,
        order,
    )
    grad_out_parts = after(tuple(grad_out_parts), grad_qkv)
    grad_out = sum(g.astype(F32) for g in grad_out_parts).astype(BF)
    grad_qkv = after(grad_qkv, grad_out)

    grad_qkv = after(grad_qkv, got_fc, got_proj, mlp_far)
    keep_qkv, give_qkv = qkv_weights(first_all, grad_qkv, [grad_out], high, dp_size)
    got_qkv = swap(give_qkv, "dp", dp_bits[-1])
    own_first, chip_first, give_first, first_sums, bias_sums = kernel_call(
        first_kernel,
        "first",
        [
            shape((local_rows, model_width), BF),
            shape((local_rows, model_width), BF),
            shape((tensor_size // 2, local_rows, model_width), BF),
            shape((2, model_width), F32),
            shape((1, 3 * head_cols), F32),
        ],
        [order],
        [first_hat, full_qkv, after(grad_qkv, keep_qkv)],
        2 * capacity * model_width * 3 * head_cols,
    )
    got_first = swap(give_first, "tensor", near)
    rest = dp_bits[:-2][::-1]
    got_fc = after(got_fc, own_first)
    got_proj = after(got_proj, own_first)
    for bit in rest:
        keep_fc, give_fc = halve(keep_fc, got_fc, "dp", bit)
        got_fc = swap(give_fc, "dp", bit)
    keep_proj, give_proj = halve(keep_proj, got_proj, "dp", dp_bits[-2])
    got_proj = swap(give_proj, "dp", dp_bits[-2])
    got_first = after(got_first, keep_fc, keep_proj)
    chip_first = (chip_first.astype(F32) + got_first[1].astype(F32)).astype(BF)
    far_first = swap(chip_first, "tensor", far)
    got_proj = after(got_proj, chip_first)
    for bit in rest:
        keep_proj, give_proj = halve(keep_proj, got_proj, "dp", bit)
        got_proj = swap(give_proj, "dp", bit)
    mlp_out = mlp_parts[0].astype(F32) + mlp_near.astype(F32) + mlp_far.astype(F32)
    result = jnp.where(
        after(live_here, keep_proj)[:, None], middle + mlp_out + proj_bias, 0.0
    ).astype(BF)
    got_qkv = after(got_qkv, result)
    for k, bit in enumerate(dp_bits[:-1][::-1]):
        keep_qkv, give_qkv = halve(keep_qkv, got_qkv, "dp", bit)
        got_qkv = swap(give_qkv, "dp", bit)
        if k == 0:
            sum_fc = keep_fc[0] + after(got_fc, keep_qkv)[0].astype(F32)
            sum_proj = (keep_proj[0] + after(got_proj, keep_qkv)[0].astype(F32)).T
    far_first = after(far_first, keep_qkv)
    (grad_tokens,) = kernel_call(
        token_kernel,
        "token_gradient",
        [shape((local_rows, model_width), BF)],
        [],
        [tokens, row(norm1_gain), own_first, got_first, far_first, grad_middle],
        0,
    )

    sum_qkv = keep_qkv[0] + after(got_qkv, grad_tokens)[0].astype(F32)
    sum_out = sum_qkv[:, 3 * head_cols :].T
    sum_qkv = (
        sum_qkv[:, : 3 * head_cols]
        .reshape(shard_rows, heads, 3, HS)
        .transpose(0, 2, 1, 3)
        .reshape(shard_rows, 3, head_cols)
    )
    bias_sums = bias_sums.reshape(heads, 3, HS)[:, 0::2].transpose(1, 0, 2).reshape(2, head_cols)
    qv_full = lax.dynamic_update_slice_in_dim(
        jnp.zeros((2, model_width), F32), bias_sums, tensor_pos * head_cols, 1
    )
    fc_full = lax.dynamic_update_slice_in_dim(
        jnp.zeros(fc_bias.shape, F32),
        (sum_pre_a + sum_pre_b).reshape(-1),
        tensor_pos * hidden_cols,
        0,
    )
    small = everyone_sum(
        jnp.concatenate(
            [after(first_sums, chip_first).reshape(-1), qv_full.reshape(-1), middle_sums.reshape(-1), fc_full]
        ).reshape(-1, 128),
        ("tensor", "dp"),
    ).reshape(-1)
    w = model_width
    return (
        result,
        grad_tokens,
        small[:w],
        small[w : 2 * w],
        sum_qkv,
        small[2 * w : 4 * w].reshape(2, w),
        sum_out,
        small[4 * w : 5 * w],
        small[5 * w : 6 * w],
        small[6 * w : 7 * w],
        sum_fc,
        small[8 * w :],
        sum_proj,
        small[7 * w : 8 * w],
    )


def solution(mesh):
    placed = (
        P(("dp", "tensor"), None),
        P("dp", None),
        P(),
        P(),
        P("dp", None, "tensor"),
        P(),
        P("tensor", "dp"),
        P(),
        P(),
        P(),
        P("dp", "tensor"),
        P(),
        P("tensor", "dp"),
        P(),
        P(("dp", "tensor"), None),
    )
    return jax.shard_map(
        per_device,
        mesh=mesh,
        in_specs=placed,
        out_specs=(
            P(("dp", "tensor"), None),
            P(("dp", "tensor"), None),
            P(),
            P(),
            P("dp", None, "tensor"),
            P(),
            P("tensor", "dp"),
            P(),
            P(),
            P(),
            P("dp", "tensor"),
            P(),
            P("tensor", "dp"),
            P(),
        ),
        check_vma=False,
    )
```

```python
import functools

import jax
import jax.numpy as jnp
from jax import lax
from jax.experimental import pallas as pl
from jax.experimental.pallas import tpu as pltpu
from jax.sharding import PartitionSpec as P

HS = 64
BLK = 128


EPSILON = 1e-05
MASKED = -1e30
GELU_SCALE = 0.7978845608028654

BF = jnp.bfloat16
F32 = jnp.float32


def segment_ids(lengths, capacity):
    padded = (lengths + BLK - 1) // BLK * BLK
    starts = jnp.cumsum(padded, axis=1) - padded
    places = jnp.arange(capacity, dtype=jnp.int32)
    inside = (places[None, None, :] >= starts[:, :, None]) & (
        places[None, None, :] < (starts + lengths)[:, :, None]
    )
    labels = jnp.arange(lengths.shape[1], dtype=jnp.int32)[None, :, None] + 1
    return jnp.sum(jnp.where(inside, labels, 0), axis=1) - 1


def swap(value, axis, bits):
    size = lax.axis_size(axis)
    return lax.ppermute(value, axis, [(i, i ^ bits) for i in range(size)])


def bits_of(axis):
    size = lax.axis_size(axis)
    count = size.bit_length() - 1
    assert 1 << count == size
    return [1 << b for b in range(count)]


def after(value, *others):
    return lax.optimization_barrier((value, *others))[0]


def gather_step(full, axis, bit, other=None):
    high = (lax.axis_index(axis) & bit) > 0
    other = swap(full, axis, bit) if other is None else other
    return jnp.where(
        high, jnp.stack([other, full], 1), jnp.stack([full, other], 1)
    ).reshape(-1, *full.shape[1:])


def exchange(blocks, axis):
    return [b if r == 0 else swap(b, axis, r) for r, b in enumerate(blocks)]


def everyone_sum(value, axes):
    for axis in axes:
        for bit in bits_of(axis):
            value = value + swap(value, axis, bit)
    return value


def first_keys(seg, slots):
    places = jnp.arange(seg.shape[0], dtype=jnp.int32)
    begins = jnp.where(seg != jnp.concatenate([jnp.full((1,), -2, jnp.int32), seg[:-1]]), places, 0)
    labels = jnp.arange(slots, dtype=jnp.int32)
    starts = jnp.sum(jnp.where((seg[None] == labels[:, None]), begins[None], 0), axis=1)
    mine = jnp.sum(jnp.where(seg[:, None] == labels[None], starts[None], 0), axis=1)
    return jnp.where(seg >= 0, mine, places)


def nt(a, b):
    return lax.dot_general(a, b, (((1,), (1,)), ((), ())), preferred_element_type=F32)


def nn(a, b):
    return lax.dot_general(a, b, (((1,), (0,)), ((), ())), preferred_element_type=F32)


def tn(a, b):
    return lax.dot_general(a, b, (((0,), (0,)), ((), ())), preferred_element_type=F32)


def rows_at(block, size):
    return pl.ds(pl.multiple_of(block * size, size), size)


def masked_scores(keys, queries, low, first_key, first_query):
    scores = nt(keys, queries)
    key_at = lax.broadcasted_iota(jnp.int32, scores.shape, 0) + first_key
    query_at = lax.broadcasted_iota(jnp.int32, (1, scores.shape[1]), 1) + first_query
    return jnp.where((key_at >= low) & (key_at <= query_at), scores, MASKED)


def forward_kernel(heads, block, here_ref, start_ref, low_ref, *refs):
    count = here_ref.shape[0] - 1
    token_refs = refs[:count]
    weight_ref, bias_ref, gain_ref, shift_ref = refs[count : count + 4]
    h1_ref, hat_ref, q_ref, k_ref, v_ref, out_ref, lse_ref = refs[count + 4 : count + 11]
    send_refs, token_all = refs[count + 11 : -1], refs[-1]
    here = here_ref[count]
    local_rows = token_refs[0].shape[0]
    chunk = 512
    for r in range(count):
        token_all[r] = token_refs[r][...]
    if True:

        def project(step, carry):
            r, part = step // (local_rows // chunk), step % (local_rows // chunk)
            base = pl.multiple_of(here_ref[r] * local_rows + part * chunk, chunk)
            rows = token_all[r, rows_at(part, chunk), :].astype(F32)
            centre = rows - jnp.mean(rows, axis=-1, keepdims=True)
            spread = jnp.mean(centre * centre, axis=-1, keepdims=True)
            hat = centre * lax.rsqrt(spread + EPSILON)
            h1 = (hat * gain_ref[...] + shift_ref[...]).astype(BF)
            hat_ref[pl.ds(base, chunk), :] = hat.astype(BF)
            h1_ref[pl.ds(base, chunk), :] = h1
            qkv = (nn(h1, weight_ref[:, : 3 * heads * HS]) + bias_ref[...]).astype(BF)
            for h in range(heads):
                at = 3 * h * HS
                q_ref[h, pl.ds(base, chunk), :] = qkv[:, at : at + HS] * HS ** (-0.5)
                k_ref[h, pl.ds(base, chunk), :] = qkv[:, at + HS : at + 2 * HS]
                v_ref[h, pl.ds(base, chunk), :] = qkv[:, at + 2 * HS : at + 3 * HS]
            return carry

        lax.fori_loop(0, count * local_rows // chunk, project, 0)

    blocks = q_ref.shape[1] // block

    def query_step(i, carry):
        low = low_ref[0:1, rows_at(i, block)]

        def key_step(j, state):
            fresh = []
            for h in range(heads):
                peak, total, acc = state[3 * h : 3 * h + 3]
                scores = masked_scores(
                    k_ref[h, rows_at(j, block), :],
                    q_ref[h, rows_at(i, block), :],
                    low,
                    j * block,
                    i * block,
                )
                peak_now = jnp.maximum(peak, jnp.max(scores, axis=0, keepdims=True))
                decay = jnp.exp(peak - peak_now)
                weights = jnp.exp(scores - peak_now)
                total = total * decay + jnp.sum(weights, axis=0, keepdims=True)
                acc = acc * decay + tn(v_ref[h, rows_at(j, block), :], weights.astype(BF))
                fresh += [peak_now, total, acc]
            return tuple(fresh)

        init = (
            jnp.full((1, block), MASKED, F32),
            jnp.zeros((1, block), F32),
            jnp.zeros((HS, block), F32),
        ) * heads
        state = lax.fori_loop(start_ref[i], i + 1, key_step, init)
        slot = lax.bitwise_xor(i, here)
        for h in range(heads):
            peak, total, acc = state[3 * h : 3 * h + 3]
            rows = acc / total
            out_ref[h, :, rows_at(i, block)] = rows
            lse_ref[h, :, rows_at(i, block)] = peak + jnp.log(total)
            for r in range(count):

                @pl.when(slot == r)
                def _(r=r, h=h, rows=rows):
                    send_refs[r][h * HS : (h + 1) * HS, :] = rows.astype(BF)

        return carry

    lax.fori_loop(0, blocks, query_step, 0)


def attention_forward(blocks, weight, bias, gain, shift, low, starts, order, heads):
    rows, width = blocks[0].shape
    count = len(blocks)
    total = rows * count
    flops = 2 * total * width * weight.shape[1] + 2 * heads * total * total * HS
    return pl.pallas_call(
        functools.partial(forward_kernel, heads, rows),
        out_shape=(
            shape((total, width), BF),
            shape((total, width), BF),
            shape((heads, total, HS), BF),
            shape((heads, total, HS), BF),
            shape((heads, total, HS), BF),
            shape((heads, HS, total), F32),
            shape((heads, 1, total), F32),
        )
        + (shape((heads * HS, rows), BF),) * count,
        in_specs=[pl.BlockSpec(memory_space=pltpu.SMEM)] * 2
        + [pl.BlockSpec(memory_space=pltpu.VMEM)] * (count + 5),
        out_specs=[pl.BlockSpec(memory_space=pltpu.VMEM)] * (7 + count),
        scratch_shapes=[pltpu.VMEM((count, rows, width), BF)],
        compiler_params=pltpu.CompilerParams(vmem_limit_bytes=60000 * 1024),
        cost_estimate=pl.CostEstimate(
            flops=flops, bytes_accessed=24 << 20, transcendentals=heads * total * total // 2
        ),
        name="attention_forward",
    )(order, starts, low, *blocks, weight, bias, gain, shift)


def backward_kernel(
    first_head, heads, block, start_ref, order_ref, low_ref, q_ref, k_ref, v_ref, out_ref, lse_ref, *refs
):
    count = order_ref.shape[0] - 1
    grad_refs = refs[:count]
    result_ref = refs[count]
    grad_t_ref, grad_ref, centre_ref, dk_ref, dv_ref, kt_ref, dq_ref = refs[count + 1 :]
    for r in range(count):
        for h in range(heads):
            whole = first_head + h
            piece = grad_refs[r][whole * HS : (whole + 1) * HS, :]
            at = rows_at(order_ref[r], block)
            grad_t_ref[h, :, at] = piece
            grad_ref[h, at, :] = piece.T
            centre_ref[h, :, at] = jnp.sum(
                piece.astype(F32) * out_ref[whole, :, at], axis=0, keepdims=True
            )
            kt_ref[h, :, r * block : (r + 1) * block] = k_ref[
                whole, r * block : (r + 1) * block, :
            ].T
    dk_ref[...] = jnp.zeros_like(dk_ref)
    dv_ref[...] = jnp.zeros_like(dv_ref)
    blocks = q_ref.shape[1] // block

    def query_step(i, carry):
        here = rows_at(i, block)
        low = low_ref[0:1, here]

        def key_step(j, state):
            there = rows_at(j, block)
            fresh = []
            for h in range(heads):
                whole = first_head + h
                queries = q_ref[whole, here, :]
                scores = masked_scores(k_ref[whole, there, :], queries, low, j * block, i * block)
                probs = jnp.exp(scores - lse_ref[whole, :, here])
                grad_probs = nn(v_ref[whole, there, :], grad_t_ref[h, :, here])
                grad_scores = (probs * (grad_probs - centre_ref[h, :, here])).astype(BF)
                dv_ref[h, there, :] += nn(probs.astype(BF), grad_ref[h, here, :])
                dk_ref[h, there, :] += nn(grad_scores, queries)
                fresh.append(state[h] + nn(kt_ref[h, :, there], grad_scores))
            return tuple(fresh)

        state = lax.fori_loop(
            start_ref[i], i + 1, key_step, (jnp.zeros((HS, block), F32),) * heads
        )
        for h in range(heads):
            dq_ref[h, here, :] = (state[h] * HS ** (-0.5)).T.astype(BF)
        return carry

    lax.fori_loop(0, blocks, query_step, 0)

    def finish(i, carry):
        here = rows_at(i, block)
        pieces = []
        for h in range(heads):
            pieces += [dq_ref[h, here, :], dk_ref[h, here, :].astype(BF), dv_ref[h, here, :].astype(BF)]
        result_ref[here, :] = jnp.concatenate(pieces, axis=1)
        return carry

    lax.fori_loop(0, blocks, finish, 0)


def vmem(count):
    return [pl.BlockSpec(memory_space=pltpu.VMEM)] * count


def smem(count):
    return [pl.BlockSpec(memory_space=pltpu.SMEM)] * count


def kernel_call(body, name, out_shape, scalars, arrays, flops, scratch=(), transcendentals=0):
    moved = sum(a.size * a.dtype.itemsize for a in arrays) + sum(
        o.size * jnp.dtype(o.dtype).itemsize for o in out_shape
    )
    return pl.pallas_call(
        body,
        out_shape=tuple(out_shape),
        in_specs=smem(len(scalars)) + vmem(len(arrays)),
        out_specs=vmem(len(out_shape)),
        scratch_shapes=list(scratch),
        compiler_params=pltpu.CompilerParams(vmem_limit_bytes=60000 * 1024),
        cost_estimate=pl.CostEstimate(
            flops=flops, bytes_accessed=moved, transcendentals=transcendentals
        ),
        name=name,
    )(*scalars, *arrays)


def shape(dims, kind):
    return jax.ShapeDtypeStruct(dims, kind)


def attention_backward(first_head, heads, q, k, v, out, lse, grads, low, starts, order):
    total = q.shape[1]
    rows = total // len(grads)
    return kernel_call(
        functools.partial(backward_kernel, first_head, heads, rows),
        "attention_backward",
        [shape((total, 3 * HS * heads), BF)],
        [starts, order],
        [low, q, k, v, out, lse, *grads],
        5 * heads * total * total * HS,
        [
            pltpu.VMEM((heads, HS, total), BF),
            pltpu.VMEM((heads, total, HS), BF),
            pltpu.VMEM((heads, 1, total), F32),
            pltpu.VMEM((heads, total, HS), F32),
            pltpu.VMEM((heads, total, HS), F32),
            pltpu.VMEM((heads, HS, total), BF),
            pltpu.VMEM((heads, total, HS), BF),
        ],
        heads * total * total // 2,
    )


def normalised(rows):
    centre = rows - jnp.mean(rows, axis=-1, keepdims=True)
    spread = jnp.mean(centre * centre, axis=-1, keepdims=True)
    scale = lax.rsqrt(spread + EPSILON)
    return centre * scale, scale


def norm_back(grad, gain, hat, scale):
    e = grad * gain
    return scale * (
        e - jnp.mean(e, axis=-1, keepdims=True) - hat * jnp.mean(e * hat, axis=-1, keepdims=True)
    )


def turn_kernel(packed_ref, out_ref):
    out_ref[...] = packed_ref[:, packed_ref.shape[1] - out_ref.shape[0] :].T


def branch_kernel(count, *refs):
    att_refs, weight_refs = refs[:count], refs[count : 2 * count]
    token_ref, bias_ref, gain_ref, shift_ref, middle_ref, h2_ref = refs[2 * count :]
    branch = bias_ref[...]
    for att, weight in zip(att_refs, weight_refs, strict=True):
        branch = branch + nn(att[...].T, weight[...])
    middle = token_ref[...].astype(F32) + branch
    middle_ref[...] = middle
    hat, _ = normalised(middle)
    h2_ref[...] = (hat * gain_ref[...] + shift_ref[...]).astype(BF)


def hidden_kernel(count, chunk, *refs):
    h2_refs, grad_refs = refs[:count], refs[count : 2 * count]
    packed_ref, bias_ref = refs[2 * count : 2 * count + 2]
    back_refs = refs[2 * count + 2 : 3 * count + 2]
    act_ref, pre_ref, sum_ref, h2_all, grad_all = refs[3 * count + 2 :]
    rows, cols = h2_refs[0].shape[0], packed_ref.shape[1] // 2
    fc_ref, proj_ref = packed_ref.at[:, :cols], packed_ref.at[:, cols:]
    sum_ref[...] = jnp.zeros_like(sum_ref)
    for r in range(count):
        h2_all[r] = h2_refs[r][...]
        grad_all[r] = grad_refs[r][...]

    def step(i, carry):
        r = i // (rows // chunk)
        at = rows_at(i % (rows // chunk), chunk)
        u = nn(h2_all[r, at, :], fc_ref[...]) + bias_ref[...]
        grad_act = nn(grad_all[r, at, :], proj_ref[...])
        square = u * u
        bend = jnp.tanh(GELU_SCALE * (u + 0.044715 * square * u))
        act_ref[r, at, :] = (0.5 * u * (1.0 + bend)).astype(BF)
        slope = 0.5 * (1.0 + bend) + 0.5 * u * (1.0 - bend * bend) * GELU_SCALE * (
            1.0 + 3.0 * 0.044715 * square
        )
        grad_pre = (grad_act * slope).astype(BF)
        pre_ref[r, at, :] = grad_pre
        sum_ref[...] += jnp.sum(grad_pre.astype(F32), axis=0, keepdims=True)
        back = nt(grad_pre, fc_ref[...]).astype(BF)
        for k in range(count):

            @pl.when(r == k)
            def _(k=k, back=back, at=at):
                back_refs[k][at, :] = back

        return carry

    lax.fori_loop(0, count * rows // chunk, step, 0)


def hidden(h2s, grads, packed, bias):
    count = len(h2s)
    rows, width = h2s[0].shape
    cols = packed.shape[1] // 2
    return kernel_call(
        functools.partial(hidden_kernel, count, 512),
        "hidden",
        [shape((rows, width), BF)] * count
        + [shape((count, rows, cols), BF)] * 2
        + [shape((1, cols), F32)],
        [],
        [*h2s, *grads, packed, bias],
        6 * count * rows * width * cols,
        [pltpu.VMEM((count, rows, width), BF)] * 2,
        transcendentals=count * rows * cols,
    )


def split_store(value, keep_ref, give_ref, high, lanes):
    pairs, rows, _ = keep_ref.shape
    for p in range(pairs):
        lower = value[2 * p * rows : (2 * p + 1) * rows, :]
        upper = value[(2 * p + 1) * rows : (2 * p + 2) * rows, :]
        keep_ref[p, :, lanes] = jnp.where(high, upper, lower)
        give_ref[p, :, lanes] = jnp.where(high, lower, upper).astype(BF)


def weight_kernel(count, high_ref, *refs):
    left_refs, right_refs = refs[:count], refs[count:-2]
    keep_ref, give_ref = refs[-2:]
    each = count // len(right_refs)
    total = tn(left_refs[0][...], right_refs[0][0])
    for r in range(1, count):
        total = total + tn(left_refs[r][...], right_refs[r // each][r % each])
    split_store(total, keep_ref, give_ref, high_ref[0] > 0, slice(0, total.shape[1]))


def hidden_weights(lefts, rights, high, dp_size):
    rows, width = lefts[0].shape
    cols = rights[0].shape[2]
    dims = (dp_size // 2, width // dp_size, cols)
    return kernel_call(
        functools.partial(weight_kernel, len(lefts)),
        "hidden_weights",
        [shape(dims, F32), shape(dims, BF)],
        [high],
        [*lefts, *rights],
        2 * len(lefts) * rows * width * cols,
    )


def project_kernel(count, *refs):
    act_refs, proj_ref, out_refs = refs[: -count - 1], refs[-count - 1], refs[-count:]
    each = count // len(act_refs)
    for r, out in enumerate(out_refs):
        act = act_refs[r // each].at[r % each]
        out[...] = nt(act[...], proj_ref[:, act.shape[1] :]).astype(BF)


def project(acts, packed):
    each, rows, cols = acts[0].shape
    width = packed.shape[0]
    count = each * len(acts)
    return kernel_call(
        functools.partial(project_kernel, count),
        "project",
        [shape((rows, width), BF)] * count,
        [],
        [*acts, packed],
        2 * count * rows * cols * width,
    )


def middle_kernel(count, middle_ref, live_grad_ref, own_ref, near_ref, far_ref, gain_ref, *refs):
    weight_refs = refs[:count]
    grad_ref, branch_ref, sums_ref = refs[count : count + 3]
    att_refs = refs[count + 3 :]
    hat, scale = normalised(middle_ref[...])
    grad = own_ref[...].astype(F32) + near_ref[...].astype(F32) + far_ref[...].astype(F32)
    here = live_grad_ref[...].astype(F32)
    total = here + norm_back(grad, gain_ref[...], hat, scale)
    grad_ref[...] = total
    branch = total.astype(BF)
    branch_ref[...] = branch
    sums_ref[0:1, :] = jnp.sum(branch.astype(F32), axis=0, keepdims=True)
    sums_ref[1:2, :] = jnp.sum(grad * hat, axis=0, keepdims=True)
    sums_ref[2:3, :] = jnp.sum(grad, axis=0, keepdims=True)
    sums_ref[3:4, :] = jnp.sum(here, axis=0, keepdims=True)
    for weight, att in zip(weight_refs, att_refs, strict=True):
        att[...] = nt(branch, weight[...]).T.astype(BF)


def out_weight_kernel(count, branch_ref, *refs):
    for att, out in zip(refs[:count], refs[count:], strict=True):
        out[...] = nn(att[...], branch_ref[...]).astype(BF)


def first_kernel(
    order_ref, hat_ref, weight_ref, part_ref, own_ref, far_ref, give_ref, sums_ref, bias_ref
):
    rows, cols = own_ref.shape[0], part_ref.shape[1]
    sums_ref[...] = jnp.zeros_like(sums_ref)
    bias_ref[...] = jnp.zeros_like(bias_ref)

    def step(r, carry):
        at = rows_at(order_ref[r], rows)
        part = part_ref[at, :]
        bias_ref[...] += jnp.sum(part.astype(F32), axis=0, keepdims=True)
        total = nt(part, weight_ref[:, :cols])
        sums_ref[0:1, :] += jnp.sum(total * hat_ref[at, :].astype(F32), axis=0, keepdims=True)
        sums_ref[1:2, :] += jnp.sum(total, axis=0, keepdims=True)
        done = total.astype(BF)

        @pl.when(r == 0)
        def _():
            own_ref[...] = done

        @pl.when(r == 2)
        def _():
            far_ref[...] = done

        @pl.when((r & 1) == 1)
        def _():
            give_ref[r // 2] = done

        return carry

    lax.fori_loop(0, 4, step, 0)


def qkv_weight_kernel(count, high_ref, h1_ref, part_ref, *refs):
    out_refs = refs[:count]
    keep_ref, give_ref = refs[count:]
    high = high_ref[0] > 0
    cols = part_ref.shape[1]
    split_store(tn(h1_ref[...], part_ref[...]), keep_ref, give_ref, high, slice(0, cols))
    total = out_refs[0][...].astype(F32).T
    split_store(total, keep_ref, give_ref, high, slice(cols, cols + total.shape[1]))


def qkv_weights(h1, part, outs, high, dp_size):
    total, width = h1.shape
    dims = (dp_size // 2, width // dp_size, part.shape[1] + outs[0].shape[0])
    return kernel_call(
        functools.partial(qkv_weight_kernel, len(outs)),
        "qkv_weights",
        [shape(dims, F32), shape(dims, BF)],
        [high],
        [h1, part, *outs],
        2 * total * width * part.shape[1],
    )


def halve_kernel(high_ref, keep_ref, got_ref, keep_out, give_out):
    high = high_ref[0] > 0
    for p in range(keep_out.shape[0]):
        lower = keep_ref[2 * p] + got_ref[2 * p].astype(F32)
        upper = keep_ref[2 * p + 1] + got_ref[2 * p + 1].astype(F32)
        keep_out[p] = jnp.where(high, upper, lower)
        give_out[p] = jnp.where(high, lower, upper).astype(BF)


def halve(keep, got, axis, bit):
    dims = (keep.shape[0] // 2, *keep.shape[1:])
    high = jnp.reshape((lax.axis_index(axis) & bit) // bit, (1,)).astype(jnp.int32)
    return kernel_call(
        halve_kernel,
        "halve",
        [shape(dims, F32), shape(dims, BF)],
        [high],
        [keep, got],
        3 * keep.size,
    )


def token_kernel(token_ref, gain_ref, own_ref, near_ref, far_ref, middle_ref, out_ref):
    hat, scale = normalised(token_ref[...].astype(F32))
    grad = own_ref[...].astype(F32) + near_ref[0].astype(F32) + far_ref[...].astype(F32)
    out_ref[...] = (middle_ref[...] + norm_back(grad, gain_ref[...], hat, scale)).astype(BF)


def per_device(
    tokens,
    seq_lengths,
    norm1_gain,
    norm1_shift,
    qkv_weight,
    qv_bias,
    out_weight,
    out_bias,
    norm2_gain,
    norm2_shift,
    fc_weight,
    fc_bias,
    proj_weight,
    proj_bias,
    out_grad,
):
    tensor_size = lax.axis_size("tensor")
    assert tensor_size == 4
    near, far = 1, 2
    dp_size = lax.axis_size("dp")
    tensor_pos = lax.axis_index("tensor")
    local_rows, model_width = tokens.shape
    capacity = local_rows * tensor_size
    shard_rows = qkv_weight.shape[0]
    head_cols = qkv_weight.shape[2]
    heads = head_cols // HS
    hidden_cols = fc_weight.shape[1]
    high = jnp.reshape(lax.axis_index("dp") & 1, (1,)).astype(jnp.int32)

    def row(vector):
        return vector.reshape(1, -1)

    qkv_heads = qkv_weight.reshape(shard_rows, 3, heads, HS).transpose(0, 2, 1, 3)
    ahead = jnp.concatenate([qkv_heads.reshape(shard_rows, -1), out_weight.T], 1)[None]
    later = jnp.concatenate([fc_weight, proj_weight.T], 1)[None]
    far_tokens = swap(tokens, "tensor", far)
    dp_bits = bits_of("dp")[::-1]
    for k, bit in enumerate(dp_bits):
        if k == len(dp_bits) - 1:
            ahead = after(ahead, far_tokens)
        ahead = gather_step(ahead, "dp", bit)
        if k == len(dp_bits) - 2:
            for early in dp_bits[:-2]:
                later = gather_step(after(later, ahead), "dp", early)
    ahead = ahead.reshape(model_width, -1)
    later_far = swap(after(later, ahead), "dp", dp_bits[-2])
    full_qkv = ahead
    (out_turned,) = kernel_call(
        turn_kernel, "turn", [shape((head_cols, model_width), BF)], [], [ahead], 0
    )
    outs = exchange([out_turned] * tensor_size, "tensor")
    near_tokens = swap(tokens, "tensor", near)
    last_tokens = swap(far_tokens, "tensor", near)
    token_blocks = [tokens, near_tokens, far_tokens, last_tokens]

    seg = segment_ids(seq_lengths, capacity)[0]
    live_here = lax.dynamic_slice_in_dim(seg, tensor_pos * local_rows, local_rows, 0) >= 0
    low = first_keys(seg, seq_lengths.shape[1])
    starts = low.reshape(tensor_size, local_rows)[:, 0] // local_rows
    order = jnp.concatenate(
        [
            lax.bitwise_xor(jnp.arange(tensor_size, dtype=jnp.int32), tensor_pos),
            jnp.reshape(tensor_pos, (1,)).astype(jnp.int32),
        ]
    )
    low = low.reshape(1, capacity)
    grad_mlp = jnp.where(live_here[:, None], out_grad, jnp.zeros_like(out_grad))
    far_grad = swap(after(grad_mlp, far_tokens), "tensor", far)
    near_grad = swap(grad_mlp, "tensor", near)

    bias_here = lax.dynamic_slice_in_dim(qv_bias, tensor_pos * head_cols, head_cols, 1).reshape(
        2, heads, HS
    )
    bias_row = row(
        jnp.stack([bias_here[0], jnp.zeros((heads, HS), F32), bias_here[1]], 1).reshape(-1)
    )
    first_all, first_hat, queries, key_rows, values, attended, log_total, *sends = attention_forward(
        token_blocks,
        full_qkv,
        bias_row,
        row(norm1_gain),
        row(norm1_shift),
        low,
        starts,
        order,
        heads,
    )

    outs = list(after(tuple(outs), sends[0]))
    sends = after(tuple(sends), far_grad, *outs)
    mine = exchange(sends, "tensor")
    later = gather_step(later, "dp", dp_bits[-2], after(later_far, sends[0]))
    later = gather_step(later, "dp", dp_bits[-1]).reshape(model_width, -1)
    last_grad = swap(after(far_grad, sends[0]), "tensor", near)
    grads = [grad_mlp, near_grad, far_grad, last_grad]
    middle, second_norm = kernel_call(
        functools.partial(branch_kernel, tensor_size),
        "branch",
        [shape((local_rows, model_width), F32), shape((local_rows, model_width), BF)],
        [],
        [*mine, *outs, tokens, row(out_bias), row(norm2_gain), row(norm2_shift)],
        2 * local_rows * model_width * model_width,
    )
    far_second = swap(second_norm, "tensor", far)
    near_second = swap(second_norm, "tensor", near)
    fc_bias_here = row(lax.dynamic_slice_in_dim(fc_bias, tensor_pos * hidden_cols, hidden_cols, 0))
    back_0, back_1, act_a, pre_a, sum_pre_a = hidden(
        [second_norm, near_second], grads[:2], later, fc_bias_here
    )
    far_second = after(far_second, back_0)
    last_second = swap(far_second, "tensor", near)
    back_2, back_3, act_b, pre_b, sum_pre_b = hidden(
        [far_second, last_second], grads[2:], later, fc_bias_here
    )
    near_back = swap(back_1, "tensor", near)
    last_back = swap(back_3, "tensor", near)
    chip_back = (back_2.astype(F32) + last_back.astype(F32)).astype(BF)
    far_back = swap(chip_back, "tensor", far)
    act_a, act_b = after((act_a, act_b), chip_back)
    acts = [act_a, act_b]
    pres = [pre_a, pre_b]
    keep_fc, give_fc = hidden_weights(
        [second_norm, near_second, far_second, last_second], pres, high, dp_size
    )
    got_fc = swap(give_fc, "dp", dp_bits[-1])
    keep_proj, give_proj = hidden_weights(
        [after(grads[0], keep_fc), *grads[1:]], acts, high, dp_size
    )
    got_proj = swap(give_proj, "dp", dp_bits[-1])
    mlp_parts = project(acts, after(later, keep_proj))
    mlp_near = swap(mlp_parts[1], "tensor", near)
    mlp_last = swap(mlp_parts[3], "tensor", near)
    mlp_far_sum = (mlp_parts[2].astype(F32) + mlp_last.astype(F32)).astype(BF)

    grad_middle, grad_branch, middle_sums, *grad_mine = kernel_call(
        functools.partial(middle_kernel, tensor_size),
        "middle",
        [
            shape((local_rows, model_width), F32),
            shape((local_rows, model_width), BF),
            shape((4, model_width), F32),
        ]
        + [shape((head_cols, local_rows), BF)] * tensor_size,
        [],
        [middle, grad_mlp, back_0, near_back, after(far_back, mlp_parts[0]), row(norm2_gain), *outs],
        2 * local_rows * model_width * model_width,
    )
    grad_attended = exchange(grad_mine, "tensor")
    mlp_far = swap(after(mlp_far_sum, grad_middle), "tensor", far)
    grad_out_parts = kernel_call(
        functools.partial(out_weight_kernel, tensor_size),
        "out_weights",
        [shape((head_cols, model_width), BF)] * tensor_size,
        [],
        [after(grad_branch, mlp_far_sum), *mine],
        2 * local_rows * model_width * model_width,
    )
    keep_fc, give_fc = halve(keep_fc, after(got_fc, grad_out_parts[0]), "dp", dp_bits[-2])
    got_fc = swap(give_fc, "dp", dp_bits[-2])
    grad_out_parts = exchange(grad_out_parts, "tensor")
    (grad_qkv,) = attention_backward(
        0,
        heads,
        queries,
        key_rows,
        values,
        attended,
        log_total,
        grad_attended,
        after(low, keep_fc),
        starts,
        order,
    )
    grad_out_parts = after(tuple(grad_out_parts), grad_qkv)
    grad_out = sum(g.astype(F32) for g in grad_out_parts).astype(BF)
    grad_qkv = after(grad_qkv, grad_out)

    grad_qkv = after(grad_qkv, got_fc, got_proj, mlp_far)
    keep_qkv, give_qkv = qkv_weights(first_all, grad_qkv, [grad_out], high, dp_size)
    got_qkv = swap(give_qkv, "dp", dp_bits[-1])
    own_first, chip_first, give_first, first_sums, bias_sums = kernel_call(
        first_kernel,
        "first",
        [
            shape((local_rows, model_width), BF),
            shape((local_rows, model_width), BF),
            shape((tensor_size // 2, local_rows, model_width), BF),
            shape((2, model_width), F32),
            shape((1, 3 * head_cols), F32),
        ],
        [order],
        [first_hat, full_qkv, after(grad_qkv, keep_qkv)],
        2 * capacity * model_width * 3 * head_cols,
    )
    got_first = swap(give_first, "tensor", near)
    rest = dp_bits[:-2][::-1]
    got_fc = after(got_fc, own_first)
    got_proj = after(got_proj, own_first)
    for bit in rest:
        keep_fc, give_fc = halve(keep_fc, got_fc, "dp", bit)
        got_fc = swap(give_fc, "dp", bit)
    keep_proj, give_proj = halve(keep_proj, got_proj, "dp", dp_bits[-2])
    got_proj = swap(give_proj, "dp", dp_bits[-2])
    got_first = after(got_first, keep_fc, keep_proj)
    chip_first = (chip_first.astype(F32) + got_first[1].astype(F32)).astype(BF)
    far_first = swap(chip_first, "tensor", far)
    got_proj = after(got_proj, chip_first)
    for bit in rest:
        keep_proj, give_proj = halve(keep_proj, got_proj, "dp", bit)
        got_proj = swap(give_proj, "dp", bit)
    mlp_out = mlp_parts[0].astype(F32) + mlp_near.astype(F32) + mlp_far.astype(F32)
    result = jnp.where(
        after(live_here, keep_proj)[:, None], middle + mlp_out + proj_bias, 0.0
    ).astype(BF)
    got_qkv = after(got_qkv, result)
    for k, bit in enumerate(dp_bits[:-1][::-1]):
        keep_qkv, give_qkv = halve(keep_qkv, got_qkv, "dp", bit)
        got_qkv = swap(give_qkv, "dp", bit)
        if k == 0:
            sum_fc = keep_fc[0] + after(got_fc, keep_qkv)[0].astype(F32)
            sum_proj = (keep_proj[0] + after(got_proj, keep_qkv)[0].astype(F32)).T
    far_first = after(far_first, keep_qkv)
    (grad_tokens,) = kernel_call(
        token_kernel,
        "token_gradient",
        [shape((local_rows, model_width), BF)],
        [],
        [tokens, row(norm1_gain), own_first, got_first, far_first, grad_middle],
        0,
    )

    sum_qkv = keep_qkv[0] + after(got_qkv, grad_tokens)[0].astype(F32)
    sum_out = sum_qkv[:, 3 * head_cols :].T
    sum_qkv = (
        sum_qkv[:, : 3 * head_cols]
        .reshape(shard_rows, heads, 3, HS)
        .transpose(0, 2, 1, 3)
        .reshape(shard_rows, 3, head_cols)
    )
    bias_sums = bias_sums.reshape(heads, 3, HS)[:, 0::2].transpose(1, 0, 2).reshape(2, head_cols)
    qv_full = lax.dynamic_update_slice_in_dim(
        jnp.zeros((2, model_width), F32), bias_sums, tensor_pos * head_cols, 1
    )
    fc_full = lax.dynamic_update_slice_in_dim(
        jnp.zeros(fc_bias.shape, F32),
        (sum_pre_a + sum_pre_b).reshape(-1),
        tensor_pos * hidden_cols,
        0,
    )
    small = everyone_sum(
        jnp.concatenate(
            [after(first_sums, chip_first).reshape(-1), qv_full.reshape(-1), middle_sums.reshape(-1), fc_full]
        ).reshape(-1, 128),
        ("tensor", "dp"),
    ).reshape(-1)
    w = model_width
    return (
        result,
        grad_tokens,
        small[:w],
        small[w : 2 * w],
        sum_qkv,
        small[2 * w : 4 * w].reshape(2, w),
        sum_out,
        small[4 * w : 5 * w],
        small[5 * w : 6 * w],
        small[6 * w : 7 * w],
        sum_fc,
        small[8 * w :],
        sum_proj,
        small[7 * w : 8 * w],
    )


def solution(mesh):
    placed = (
        P(("dp", "tensor"), None),
        P("dp", None),
        P(),
        P(),
        P("dp", None, "tensor"),
        P(),
        P("tensor", "dp"),
        P(),
        P(),
        P(),
        P("dp", "tensor"),
        P(),
        P("tensor", "dp"),
        P(),
        P(("dp", "tensor"), None),
    )
    return jax.shard_map(
        per_device,
        mesh=mesh,
        in_specs=placed,
        out_specs=(
            P(("dp", "tensor"), None),
            P(("dp", "tensor"), None),
            P(),
            P(),
            P("dp", None, "tensor"),
            P(),
            P("tensor", "dp"),
            P(),
            P(),
            P(),
            P("dp", "tensor"),
            P(),
            P("tensor", "dp"),
            P(),
        ),
        check_vma=False,
    )
```
